256 devices in a mesh: section: 8 (over y, core), seq: 32 (over x, z).
Axes of the slice: x: 4, y: 4, z: 8, core: 2. Of those that a mesh axis runs over, the one named last changes fastest.
Arguments:
- resident_microbatch: bfloat16 [8, 4096, 1024], P('section', 'seq'), may hold values from -36 to 36
- upcoming_amino_ids: int32 [4096], P('seq'), may hold values from 0 to 31
- upcoming_polymer_sizes: int32 [8], replicated, may hold values from 1 to 1024, 4096 in all
- amino_acid_vectors: bfloat16 [32, 1024], replicated, may hold values from -36 to 36
- polymer_vectors: bfloat16 [8, 1024], replicated, may hold values from -3 to 3
- normalizer_scaling: float32 [8, 1024], P('section'), may hold values from 0.25 to 1.75
- entry_projection_matrix: bfloat16 [8, 1024, 3072], P('section'), may hold values from -0.1875 to 0.1875
- convolution_kernels_long: float32 [8, 2, 1024, 4096], P('section', None, 'seq'), may hold values from -4 to 4
- convolution_skip_coefficients: float32 [8, 2, 1024], P('section', None, 'seq'), may hold values from -1 to 1
- exit_projection_matrix: bfloat16 [8, 1024, 1024], P('section'), may hold values from -0.1875 to 0.1875
- adjoint_seeds: bfloat16 [8, 2, 4096, 1024], P('section', None, 'seq'), may hold values from -0.0625 to 0.0625
Outputs:
- passed: bfloat16 [8, 4096, 1024], P('section', 'seq')
- out_grad: float32 [8, 1024, 1024], P('section', 'seq')
The draws below stay inside these ranges and needn't reach their ends.
All inputs are finite; a program needn't handle non-finite values.
Results may differ from the reference program's by a relative error of at most 0.025.
Values may be sent and summed in bfloat16 or wider, within the bound.
A program may use at most 128 MiB of HBM per device.

```python
import math
import jax
import jax.numpy as jnp
import numpy as np
from jax import lax

D = 1024
VOCAB = 32
CHAINS = 8
SEQ_DEV = 128
SECTIONS = 8
LEN = 4096
N_SEQ = 32


def scaled_field(key, lead_shape, columns):
    sub_keys = jax.random.split(key, 3)
    full_shape = lead_shape + (columns,)
    base_values = jnp.clip(jax.random.normal(sub_keys[0], full_shape, jnp.float32), -4.0, 4.0)
    row_scale = jnp.exp(jax.random.uniform(sub_keys[1], lead_shape + (1,), jnp.float32, math.log(0.3), math.log(3.0)))
    column_scale = jnp.exp(jax.random.uniform(sub_keys[2], (columns,), jnp.float32, math.log(0.3), math.log(3.0)))
    return base_values * row_scale * column_scale


def draw_resident_microbatch(key, part):
    return scaled_field(jax.random.fold_in(key, 11), (SECTIONS, LEN), D).astype(jnp.bfloat16)


def draw_amino_acid_vectors(key, part):
    return scaled_field(jax.random.fold_in(key, 23), (VOCAB,), D).astype(jnp.bfloat16)


def draw_convolution_kernels_long(key, part):
    sub_keys = jax.random.split(jax.random.fold_in(key, 37), 2)
    rate_shape = (SECTIONS, 2, D, 1)
    rates = jnp.exp(jax.random.uniform(sub_keys[0], rate_shape, jnp.float32, math.log(0.05 / LEN), math.log(1.0 / 30.0)))
    noise = jnp.clip(jax.random.normal(sub_keys[1], (SECTIONS, 2, D, LEN), jnp.float32), -4.0, 4.0)
    lags = jnp.arange(LEN, dtype=jnp.float32)
    amplitude = jnp.sqrt(jnp.expm1(-2.0 * rates) / jnp.expm1(-2.0 * rates * LEN))
    return noise * amplitude * jnp.exp(-rates * lags)


def place_ends(drawn, key, low, largest):
    spot = [jax.random.randint(jax.random.fold_in(key, axis), (), 0, length) for axis, length in enumerate(drawn.shape)]
    main_axis = drawn.shape.index(max(drawn.shape))
    neighbour = spot[:main_axis] + [(spot[main_axis] + 1) % drawn.shape[main_axis]] + spot[main_axis + 1:]
    return drawn.at[tuple(spot)].set(low).at[tuple(neighbour)].set(largest)


def level_of(rng, shape, cuts, smallest, high):
    def one(dim, parts):
        heights = jax.random.uniform(jax.random.fold_in(jax.random.fold_in(rng, 6), dim), (parts,), jnp.float32, smallest / len(cuts), high / len(cuts))
        return jnp.repeat(jnp.exp(heights), shape[dim] // parts).reshape((-1,) + (1,) * (len(shape) - dim - 1))

    level = one(*cuts[0])
    for cut in cuts[1:]:
        level = level * one(*cut)
    return level


def rank_bounds(amount, lean):
    weights = [(1 << 20) // math.isqrt(grade ** lean) + 1 for grade in range(1, amount + 1)]
    deviation = 1 + sum(weights) // (1 << 30)
    return np.cumsum(np.array([max(1, weight // deviation) for weight in weights]))


def skewed_ids(rng, dims, count, skew):
    table = rank_bounds(count, skew)
    lot = jax.random.randint(jax.random.fold_in(rng, 1), dims, 0, int(table[count - 1]))
    grade = jnp.searchsorted(jnp.asarray(table, jnp.int32), lot, side="right")
    return jax.random.permutation(jax.random.fold_in(rng, 2), count)[grade].astype(jnp.int32)


def split_up(amount, total, reach, lean):
    portions = [(1 << 20) // math.isqrt(standing ** lean) + 1 for standing in range(2, amount + 1)]
    rest, counts = total - reach - (amount - 1), [1] * (amount - 1)
    while rest > 0:
        candidates = [i for i in range(amount - 1) if counts[i] < reach]
        pool, budget = sum([portions[i] for i in candidates]), rest
        for i in candidates:
            extra = min(reach - counts[i], max(1, budget * portions[i] // pool), rest)
            counts[i] = counts[i] + extra
            rest = rest - extra
    return np.array([reach] + counts)


def ragged_sizes(own_key, amount, total, most, lean):
    if amount == 2:
        one = jax.random.randint(own_key, (), max(1, total - most), min(most, total - 1) + 1)
        return jnp.stack([one, total - one])
    lengths = jnp.asarray(split_up(amount, total, most, lean), jnp.int32)
    couples = (amount - 1) // 2
    giver, taker = lengths[1:1 + 2 * couples:2], lengths[2:2 + 2 * couples:2]
    slack = jnp.minimum(giver - 1, most - taker)
    moved = jax.random.randint(jax.random.fold_in(own_key, 1), (couples,), 0, 1 << 20) % (slack + 1)
    lengths = lengths.at[1:1 + 2 * couples:2].set(giver - moved).at[2:2 + 2 * couples:2].set(taker + moved)
    return lengths[jax.random.permutation(jax.random.fold_in(own_key, 2), amount)]


def centred(own_key, extent, width, limit, cuts=(), held_as=jnp.bfloat16):
    values = width * jax.random.normal(own_key, extent, jnp.float32)
    if cuts:
        values = values * level_of(own_key, extent, cuts, -0.22, 0.18)
    return jnp.clip(values, -limit, limit).astype(held_as)


def setup_inputs(seed: int = 0) -> dict:
    key_list = jax.random.split(jax.random.key(seed), 12)
    resident_microbatch = draw_resident_microbatch(jax.random.fold_in(key_list[11], 71), 0)
    upcoming_amino_ids = place_ends(skewed_ids(key_list[1], (LEN,), VOCAB, 2), jax.random.fold_in(key_list[1], 3), 0, VOCAB - 1).astype(jnp.int32)
    upcoming_polymer_sizes = ragged_sizes(key_list[2], CHAINS, LEN, LEN // 4, 2).astype(jnp.int32)
    amino_acid_vectors = draw_amino_acid_vectors(jax.random.fold_in(key_list[11], 71), 0)
    polymer_vectors = centred(key_list[4], (CHAINS, D), 0.5, 3.0)
    normalizer_scaling = jnp.clip(1.0 + 0.15 * jax.random.normal(key_list[5], (SECTIONS, D), jnp.float32), 0.25, 1.75)
    entry_projection_matrix = centred(key_list[6], (SECTIONS, D, 3 * D), D ** -0.5, 0.1875, ((0, 8),))
    convolution_kernels_long = draw_convolution_kernels_long(jax.random.fold_in(key_list[11], 71), 0)
    convolution_skip_coefficients = jnp.clip(jax.random.uniform(key_list[8], (SECTIONS, 2, D), jnp.float32, -1.0, 1.0) * level_of(key_list[8], (SECTIONS, 2, D), ((0, 8), (2, 32)), -0.4, 0.0), -1.0, 1.0)
    exit_projection_matrix = centred(key_list[9], (SECTIONS, D, D), D ** -0.5, 0.1875, ((0, 8),))
    adjoint_seeds = centred(key_list[10], (SECTIONS, 2, LEN, D), 0.01, 0.0625, ((0, 8), (2, 32)))
    return dict(resident_microbatch=resident_microbatch, upcoming_amino_ids=upcoming_amino_ids, upcoming_polymer_sizes=upcoming_polymer_sizes, amino_acid_vectors=amino_acid_vectors, polymer_vectors=polymer_vectors, normalizer_scaling=normalizer_scaling, entry_projection_matrix=entry_projection_matrix, convolution_kernels_long=convolution_kernels_long, convolution_skip_coefficients=convolution_skip_coefficients, exit_projection_matrix=exit_projection_matrix, adjoint_seeds=adjoint_seeds)


epsilon = 1e-06

def causal_conv(signal, kernel, skip_gain):
    seq_len = signal.shape[0]
    padded_len = 2 * seq_len
    spectrum = jnp.fft.rfft(signal, n=padded_len, axis=0) * jnp.fft.rfft(kernel.T, n=padded_len, axis=0)
    return jnp.fft.irfft(spectrum, n=padded_len, axis=0)[:seq_len] + skip_gain[None, :] * signal

def run_gated_convolution_block(inputs, gain, weight_in, kernels, skips, weight_out):
    model_width = inputs.shape[1]
    values = inputs.astype(jnp.float32)
    inverse_rms = lax.rsqrt(lax.optimization_barrier(jnp.mean(values * values, axis=1, keepdims=True)) + epsilon)
    normed = (values * inverse_rms * gain).astype(jnp.bfloat16)
    projected = jnp.dot(normed, weight_in, preferred_element_type=jnp.float32).astype(jnp.bfloat16)
    value_cols = projected[:, :model_width].astype(jnp.float32)
    gate_one = projected[:, model_width:2 * model_width].astype(jnp.float32)
    gate_two = projected[:, 2 * model_width:].astype(jnp.float32)
    gated = gate_one * causal_conv(value_cols, kernels[0], skips[0])
    mixed = causal_conv(gated, kernels[1], skips[1]).astype(jnp.bfloat16)
    hyena_rows = (gate_two * mixed.astype(jnp.float32)).astype(jnp.bfloat16)
    layer_out = (values + jnp.dot(hyena_rows, weight_out, preferred_element_type=jnp.float32)).astype(jnp.bfloat16)
    return (layer_out, hyena_rows)

def block_grad(first_y, second_y, first_cot, second_cot):
    model_width = first_y.shape[1]
    shaped = (N_SEQ, SEQ_DEV, model_width)

    def add_block(total, pieces):
        first_rows, second_rows, first_slab, second_slab = pieces
        first_term = jnp.dot(first_rows.T, first_slab, preferred_element_type=jnp.float32).astype(jnp.bfloat16)
        second_term = jnp.dot(second_rows.T, second_slab, preferred_element_type=jnp.float32).astype(jnp.bfloat16)
        first_term, second_term = lax.optimization_barrier((first_term, second_term))
        return (total + first_term.astype(jnp.float32) + second_term.astype(jnp.float32), None)
    start = jnp.zeros((model_width, model_width), jnp.float32)
    total, _ = lax.scan(add_block, start, (first_y.reshape(shaped), second_y.reshape(shaped), first_cot.reshape(shaped), second_cot.reshape(shaped)))
    return total

def reference(resident_microbatch, upcoming_amino_ids, upcoming_polymer_sizes, amino_acid_vectors, polymer_vectors, normalizer_scaling, entry_projection_matrix, convolution_kernels_long, convolution_skip_coefficients, exit_projection_matrix, adjoint_seeds):
    chain_ends = jnp.cumsum(upcoming_polymer_sizes).astype(jnp.int32)[:-1]
    position = jnp.arange(LEN, dtype=jnp.int32)
    chain_id = lax.optimization_barrier(jnp.sum((position[:, None] >= chain_ends[None, :]).astype(jnp.int32), axis=1)).astype(jnp.int32)
    embedded = (amino_acid_vectors[upcoming_amino_ids].astype(jnp.float32) + polymer_vectors[chain_id].astype(jnp.float32)).astype(jnp.bfloat16)
    initial_handover_round = []
    for device_ordinal in range(SECTIONS):
        initial_handover_round.append(run_gated_convolution_block(resident_microbatch[device_ordinal], normalizer_scaling[device_ordinal], entry_projection_matrix[device_ordinal], convolution_kernels_long[device_ordinal], convolution_skip_coefficients[device_ordinal], exit_projection_matrix[device_ordinal]))
    passed = []
    grads = []
    for device_ordinal in range(SECTIONS):
        source = embedded if device_ordinal == 0 else initial_handover_round[device_ordinal - 1][0]
        layer_out, hyena_rows = run_gated_convolution_block(source, normalizer_scaling[device_ordinal], entry_projection_matrix[device_ordinal], convolution_kernels_long[device_ordinal], convolution_skip_coefficients[device_ordinal], exit_projection_matrix[device_ordinal])
        passed.append(layer_out)
        grads.append(block_grad(initial_handover_round[device_ordinal][1], hyena_rows, adjoint_seeds[device_ordinal, 0], adjoint_seeds[device_ordinal, 1]))
    return (jnp.stack(passed), jnp.stack(grads))
```

```python
import math

import jax
import jax.numpy as jnp
import numpy as np
from jax import lax
from jax.experimental import pallas as pl
from jax.experimental.pallas import tpu as pltpu
from jax.sharding import Mesh
from jax.sharding import PartitionSpec as P

MESH = pl.DeviceIdType.MESH
F32 = jnp.float32
BF16 = jnp.bfloat16
EPS = 1e-06
LANES = 128
CH = 32


def dft_tables(blocks):
    n = LANES * blocks
    a = np.arange(blocks)[None, :]
    k1 = np.arange(blocks)[:, None]
    first = 2.0 * math.pi * a * (k1 + 0.25) / blocks
    eye = np.eye(8)
    fwd = np.kron(np.concatenate([np.cos(first), -np.sin(first)], axis=0), eye)
    inv = np.kron(np.concatenate([np.cos(first).T, -np.sin(first).T], axis=1), eye)
    q = np.arange(LANES)[None, :]
    twist = np.repeat(2.0 * math.pi * q * (k1 + 0.25) / n, 8, axis=0)
    last = 2.0 * math.pi * (np.arange(LANES)[:, None] * q % LANES) / LANES
    c, s = np.cos(last), np.sin(last)
    g_fwd = np.block([[c, -s], [s, c]])
    g_inv = np.block([[c, s], [-s, c]])
    return (
        jnp.asarray(fwd, BF16),
        jnp.asarray(inv, BF16),
        jnp.asarray(np.stack([np.cos(twist), np.sin(twist)]), F32),
        jnp.asarray(np.stack([g_fwd, g_inv]), BF16),
    )


def dot(a, b):
    return lax.dot_general(a, b, (((1,), (0,)), ((), ())), preferred_element_type=F32)


def body(ns, nx, nz,
         x_ref, ids_ref, sizes_ref, amino_ref, poly_ref, gain_ref, win_hbm, h_hbm, skip_ref, wout_hbm,
         seeds_hbm, fk_ref, fi_ref, tw_ref, g_ref,
         passed_ref, grad_ref,
         win, wout, h, spec, sall, vsend, gsend, vrecv, grecv, msend, mrecv, g2t, hyt, yall, hsend, hrecv,
         emb, tab, rsend, rrecv, part,
         lsem, a2a_s, a2a_r, sh_s, sh_r, y_s, y_r, s_s, s_r, f_s, f_r, z_s, z_r):
    seq = nx * nz
    d = CH * seq
    cw = CH * nz
    rows = 8 * seq
    sec, x, z = lax.axis_index("section"), lax.axis_index("seq_0"), lax.axis_index("seq_1")
    me = x * nz + z
    left, right = lax.rem(x + nx - 1, nx), lax.rem(x + 1, nx)
    after, before = lax.rem(sec + 1, ns), lax.rem(sec + ns - 1, ns)

    local = []
    for p in range(3):
        for j in range(nx):
            local.append(pltpu.make_async_copy(
                win_hbm.at[:, pl.ds((p * nx + j) * cw, cw)], win.at[p, j], lsem.at[p * nx + j]))
    local.append(pltpu.make_async_copy(h_hbm, h, lsem.at[3 * nx]))
    for step in range(2):
        local.append(pltpu.make_async_copy(seeds_hbm.at[step], sall.at[step, x], lsem.at[3 * nx + 1 + step]))
    for j in range(nx):
        local.append(pltpu.make_async_copy(
            wout_hbm.at[:, pl.ds(j * cw, cw)], wout.at[j], lsem.at[3 * nx + 3 + j]))
    for c in local:
        c.start()

    barrier = pltpu.get_barrier_semaphore()

    def greet(i, carry):
        peer = lax.rem(me + i, seq)
        pl.semaphore_signal(barrier, inc=1, device_id=(sec, peer // nz, lax.rem(peer, nz)), device_id_type=MESH)
        return carry

    lax.fori_loop(1, seq, greet, 0)
    pl.semaphore_signal(barrier, inc=1, device_id=(after, x, z), device_id_type=MESH)
    pl.semaphore_signal(barrier, inc=1, device_id=(before, x, z), device_id_type=MESH)

    def far(i):
        half = (i + 1) // 2
        return nz // 2 + half * (1 - 2 * lax.rem(i, 2))

    def block_copy(src, dst, s_idx, r_idx, layer, kind, peer):
        return pltpu.make_async_remote_copy(
            src_ref=src, dst_ref=dst, send_sem=a2a_s.at[layer, kind, s_idx], recv_sem=a2a_r.at[layer, kind, r_idx],
            device_id=(sec, peer // nz, lax.rem(peer, nz)), device_id_type=MESH)

    def send_column(send, recv, layer, kind, xx, own):
        def one(i, carry):
            peer = xx * nz + lax.rem(z + far(i), nz)
            block_copy(send.at[peer], recv.at[me], peer, me, layer, kind, peer).start()
            return carry

        lax.fori_loop(0, nz - 1, one, 0)
        if own:
            recv[me] = send[me]
        else:
            peer = xx * nz + z
            block_copy(send.at[peer], recv.at[me], peer, me, layer, kind, peer).start()

    def wait_blocks(send, recv, layer, kind):
        def one(i, carry):
            peer = lax.rem(me + i, seq)
            block_copy(send.at[peer], recv.at[peer], peer, peer, layer, kind, peer).wait_recv()
            return carry

        lax.fori_loop(1, seq, one, 0)

    def drain_blocks(send, recv, layer, kind):
        def one(i, carry):
            peer = lax.rem(me + i, seq)
            block_copy(send.at[peer], recv.at[peer], peer, peer, layer, kind, peer).wait_send()
            return carry

        lax.fori_loop(1, seq, one, 0)

    orders = [o % nx for o in (2, 1, 3, 0)]

    def half_m(ref, half):
        return lambda i: ref.at[i, pl.ds(16 * half, 16)]

    def send_mixed(layer, half):
        src, dst = half_m(msend, half), half_m(mrecv, half)

        def to(peer):
            block_copy(src(peer), dst(me), peer, me, layer, 2 + half, peer).start()

        for o in orders:
            xx = lax.rem(x + o, nx)

            def one(i, carry):
                to(xx * nz + lax.rem(z + far(i), nz))
                return carry

            lax.fori_loop(0, nz - 1, one, 0)
            if o:
                to(xx * nz + z)
        mrecv[me, 16 * half:16 * half + 16] = msend[me, 16 * half:16 * half + 16]

    def wait_mixed(layer, half, sent):
        src, dst = half_m(msend, half), half_m(mrecv, half)

        def one(i, carry):
            peer = lax.rem(me + i, seq)
            c = block_copy(src(peer), dst(peer), peer, peer, layer, 2 + half, peer)
            if sent:
                c.wait_send()
            else:
                c.wait_recv()
            return carry

        lax.fori_loop(1, seq, one, 0)

    def seed_copy(step, direction):
        return pltpu.make_async_remote_copy(
            src_ref=sall.at[step, x], dst_ref=sall.at[step, x], send_sem=s_s.at[step, direction],
            recv_sem=s_r.at[step, direction], device_id=(sec, (right, left)[direction], z), device_id_type=MESH)

    def seed_arrival(step, direction):
        src = (left, right)[direction]
        return pltpu.make_async_remote_copy(
            src_ref=sall.at[step, src], dst_ref=sall.at[step, src], send_sem=s_s.at[step, direction],
            recv_sem=s_r.at[step, direction], device_id=(sec, (right, left)[direction], z), device_id_type=MESH)

    def forward_copy(step, direction):
        src = (left, right)[direction]
        part_rows = pl.ds(64 * direction, 64)
        return pltpu.make_async_remote_copy(
            src_ref=sall.at[step, src, part_rows], dst_ref=sall.at[step, src, part_rows],
            send_sem=f_s.at[step, direction], recv_sem=f_r.at[step, direction],
            device_id=(sec, (right, left)[direction], z), device_id_type=MESH)

    def forward_arrival(step, direction):
        src = lax.rem(x + 2, nx)
        part_rows = pl.ds(64 * direction, 64)
        return pltpu.make_async_remote_copy(
            src_ref=sall.at[step, src, part_rows], dst_ref=sall.at[step, src, part_rows],
            send_sem=f_s.at[step, direction], recv_sem=f_r.at[step, direction],
            device_id=(sec, (right, left)[direction], z), device_id_type=MESH)

    def forward(xin):
        first = dot(fk_ref[...], xin)
        wc, ws = tw_ref[0], tw_ref[1]
        outs = []
        for k in range(2):
            re, im = first[:rows, LANES * k:LANES * k + LANES], first[rows:, LANES * k:LANES * k + LANES]
            turned = jnp.concatenate([re * wc + im * ws, im * wc - re * ws], axis=1).astype(BF16)
            outs.append(dot(turned, g_ref[0]))
        return outs

    def long_filter(xin, f, pair):
        wc, ws = tw_ref[0], tw_ref[1]
        cols = []
        for k, zz in enumerate(forward(xin)):
            s = spec[f, 2 * pair + k]
            zr, zi, hr, hi = zz[:, :LANES], zz[:, LANES:], s[:, :LANES], s[:, LANES:]
            prod = jnp.concatenate([zr * hr - zi * hi, zr * hi + zi * hr], axis=1).astype(BF16)
            back = dot(prod, g_ref[1])
            br, bi = back[:, :LANES], back[:, LANES:]
            cols.append(jnp.concatenate([br * wc - bi * ws, br * ws + bi * wc], axis=0).astype(BF16))
        return dot(fi_ref[...], jnp.concatenate(cols, axis=1))

    def rows_of(ref, pair):
        v = ref[:, 16 * pair:16 * pair + 16, :].astype(F32)
        return jnp.concatenate([v[:, :8, :].reshape(rows, LANES), v[:, 8:, :].reshape(rows, LANES)], axis=1)

    def skip_tile(f, group):
        row = lax.broadcasted_iota(jnp.int32, (8, LANES), 0)
        out = jnp.zeros((8, LANES), F32)
        for r in range(8):
            out = jnp.where(row == r, skip_ref[f, 8 * group + r], out)
        return out

    def with_skip(y, f, pair, xin):
        gains = jnp.concatenate([skip_tile(f, 2 * pair), skip_tile(f, 2 * pair + 1)], axis=1)
        return y + (xin.reshape(seq, 8, 2 * LANES) * gains[None]).reshape(rows, 2 * LANES)

    def convolve(pair):
        v = rows_of(vrecv, pair)
        y = with_skip(long_filter(v.astype(BF16), 0, pair), 0, pair, v)
        gated = rows_of(grecv, pair) * y
        y = with_skip(long_filter(gated.astype(BF16), 1, pair), 1, pair, gated)
        y = y.reshape(seq, 8, 2 * LANES)
        out = jnp.concatenate([y[:, :, :LANES], y[:, :, LANES:]], axis=1)
        msend[:, 16 * pair:16 * pair + 16, :] = out.astype(BF16)

    def filter_spectra():
        scale = 1.0 / (LANES * seq)
        for f in range(2):
            for pair in range(2):
                cols = []
                for k in range(2):
                    lo = 16 * pair + 8 * k
                    cols.append(jnp.concatenate(
                        [h[f, lo:lo + 8, LANES * a:LANES * a + LANES] for a in range(seq)], axis=0))
                outs = forward(jnp.concatenate(cols, axis=1).astype(BF16))
                for k in range(2):
                    spec[f, 2 * pair + k] = outs[k] * scale

    def embed():
        token = lax.broadcasted_iota(jnp.int32, (LANES, LANES), 0)
        pos = me * LANES + lax.broadcasted_iota(jnp.int32, (LANES, LANES), 1)
        chain = jnp.zeros((LANES, LANES), jnp.int32)
        end = jnp.int32(0)
        for j in range(7):
            end = end + sizes_ref[j]
            chain = chain + jnp.where(pos >= end, 1, 0)
        vocab = amino_ref.shape[0]
        ids = jnp.broadcast_to(ids_ref[...], (LANES, LANES))
        hot = jnp.where(token < vocab, jnp.where(token == ids, 1.0, 0.0), jnp.where(token - vocab == chain, 1.0, 0.0))
        tab[...] = jnp.zeros_like(tab)
        tab[:vocab] = amino_ref[...].astype(F32)
        tab[vocab:vocab + 8] = poly_ref[...].astype(F32)
        emb[...] = dot(hot.astype(F32).T.astype(BF16), tab[...].astype(BF16)).astype(BF16)

    def wait_win(p):
        for j in range(nx):
            local[p * nx + j].wait()

    def layer(k, values):
        normed = (values * lax.rsqrt(jnp.mean(values * values, axis=1, keepdims=True) + EPS) * gain_ref[...]).astype(BF16)
        per = cw // CH
        for p, send, recv in ((0, vsend, vrecv), (1, gsend, grecv)):
            if k == 0:
                wait_win(p)
            for o in orders:
                xx = lax.rem(x + o, nx)
                chunk = dot(normed, win[p, xx]).T.astype(BF16)
                send[pl.ds(xx * per, per)] = chunk.reshape(per, CH, LANES)
                if k == 0 and p == 0 and o == orders[0]:
                    pl.semaphore_wait(barrier, seq + 1)
                send_column(send, recv, k, p, xx, o == 0)
        if k == 0:
            wait_win(2)
        for j in range(nx):
            g2t[pl.ds(j * cw, cw)] = dot(normed, win[2, j]).T.astype(BF16)
        if k == 0:
            local[3 * nx].wait()
            filter_spectra()
            embed()
        wait_blocks(vsend, vrecv, k, 0)
        wait_blocks(gsend, grecv, k, 1)
        if k == 0:
            for step in range(2):
                local[3 * nx + 1 + step].wait()
            seed_copy(0, 0).start()
            seed_copy(0, 1).start()
        else:
            for step in range(2):
                for w in range(2):
                    seed_arrival(step, w).wait_recv()
                    forward_copy(step, w).start()
        for pair in range(2):
            convolve(pair)
            send_mixed(k, pair)
        drain_blocks(vsend, vrecv, k, 0)
        drain_blocks(gsend, grecv, k, 1)
        if k == 0:
            for j in range(nx):
                local[3 * nx + 3 + j].wait()
        else:
            for step in range(2):
                for w in range(2):
                    forward_arrival(step, w).wait_recv()
            grad_of(0)
        for half in range(2):
            wait_mixed(k, half, False)
        for half in range(2):
            wait_mixed(k, half, True)
        hyena = mrecv[...].reshape(d, LANES).astype(F32) * g2t[...].astype(F32)
        hyt[k] = hyena.astype(BF16).reshape(nx, cw, LANES)
        for o in orders:
            if o:
                y_copy(k, lax.rem(x + o, nx)).start()
        yall[k, x] = hyt[k, x]
        return hyena.T.astype(BF16)

    def y_copy(step, xx):
        return pltpu.make_async_remote_copy(
            src_ref=hyt.at[step, xx], dst_ref=yall.at[step, x], send_sem=y_s.at[step, xx], recv_sem=y_r.at[step, x],
            device_id=(sec, xx, z), device_id_type=MESH)

    def y_arrival(step, xx):
        return pltpu.make_async_remote_copy(
            src_ref=hyt.at[step, xx], dst_ref=yall.at[step, xx], send_sem=y_s.at[step, xx], recv_sem=y_r.at[step, xx],
            device_id=(sec, xx, z), device_id_type=MESH)

    def grad_of(step):
        for o in range(1, nx):
            y_arrival(step, lax.rem(x + o, nx)).wait_recv()
        y = jnp.concatenate([yall[step, j] for j in range(nx)], axis=1)
        half_d = d // 2
        for n in range(2):
            cols = slice(n * half_d, (n + 1) * half_d)
            s = jnp.concatenate([sall[step, j, :, cols] for j in range(nx)], axis=0)
            term = dot(y, s)
            if step == 0:
                part[:, cols] = term
            else:
                part[:, cols] = part[:, cols] + term

    def shift_copy(j):
        return pltpu.make_async_remote_copy(
            src_ref=hsend.at[j], dst_ref=hrecv.at[j], send_sem=sh_s.at[j], recv_sem=sh_r.at[j],
            device_id=(after, x, z), device_id_type=MESH)

    first_in = x_ref[...].astype(F32)
    hyena_rows = layer(0, first_in)
    for j in range(nx):
        out = x_ref[:, j * cw:(j + 1) * cw].astype(F32) + dot(hyena_rows, wout[j])
        hsend[j] = out.astype(BF16)
        shift_copy(j).start()
    seed_copy(1, 0).start()
    seed_copy(1, 1).start()
    for j in range(nx):
        shift_copy(j).wait_recv()
    handed = jnp.concatenate([hrecv[j] for j in range(nx)], axis=1)
    head = lax.broadcast(sec, (LANES, d)) == 0
    second_in = jnp.where(head, emb[...].astype(F32), handed.astype(F32))
    emb[...] = second_in.astype(BF16)
    hyena_rows = layer(1, second_in)
    for j in range(nx):
        cols = slice(j * cw, (j + 1) * cw)
        passed_ref[:, cols] = (emb[:, cols].astype(F32) + dot(hyena_rows, wout[j])).astype(BF16)
    grad_of(1)

    def z_copy(zz, to):
        return pltpu.make_async_remote_copy(
            src_ref=rsend.at[zz], dst_ref=rrecv.at[z if to else zz], send_sem=z_s.at[zz],
            recv_sem=z_r.at[z if to else zz], device_id=(sec, x, zz), device_id_type=MESH)

    rsend[...] = part[...].astype(BF16).reshape(nz, CH, d)

    def z_send(i, carry):
        z_copy(lax.rem(z + far(i), nz), True).start()
        return carry

    lax.fori_loop(0, nz - 1, z_send, 0)
    grad_ref[...] = part[pl.ds(pl.multiple_of(z * CH, CH), CH), :]

    for j in range(nx):
        shift_copy(j).wait_send()
    for step in range(2):
        for w in range(2):
            seed_copy(step, w).wait_send()
            forward_copy(step, w).wait_send()
        for o in range(1, nx):
            y_copy(step, lax.rem(x + o, nx)).wait_send()

    def z_wait(i, carry):
        zz = lax.rem(z + i, nz)
        z_copy(zz, False).wait_recv()
        grad_ref[...] = grad_ref[...] + rrecv[zz].astype(F32)
        return carry

    lax.fori_loop(1, nz, z_wait, 0)

    def z_drain(i, carry):
        z_copy(lax.rem(z + i, nz), True).wait_send()
        return carry

    lax.fori_loop(1, nz, z_drain, 0)


def local(shape, resident, ids, sizes, amino, poly, gain, win, kernels, skips, wout, seeds):
    ns, nx, nz = shape
    seq = nx * nz
    d = CH * seq
    cw = CH * nz
    fk, fi, tw, g = dft_tables(seq)
    vmem = pl.BlockSpec(memory_space=pltpu.VMEM)
    smem = pl.BlockSpec(memory_space=pltpu.SMEM)
    hbm = pl.BlockSpec(memory_space=pl.ANY)
    dma = pltpu.SemaphoreType.DMA
    passed, grad = pl.pallas_call(
        lambda *refs: body(ns, nx, nz, *refs),
        out_shape=(jax.ShapeDtypeStruct((LANES, d), BF16), jax.ShapeDtypeStruct((CH, d), F32)),
        in_specs=[vmem, vmem, smem, vmem, vmem, vmem, hbm, hbm, smem, hbm, hbm, vmem, vmem, vmem, vmem],
        out_specs=(vmem, vmem),
        scratch_shapes=[
            pltpu.VMEM((3, nx, d, cw), BF16),
            pltpu.VMEM((nx, d, cw), BF16),
            pltpu.VMEM((2, CH, LANES * seq), F32),
            pltpu.VMEM((2, 4, 8 * seq, 2 * LANES), F32),
            pltpu.VMEM((2, nx, LANES, d), BF16),
            pltpu.VMEM((seq, CH, LANES), BF16),
            pltpu.VMEM((seq, CH, LANES), BF16),
            pltpu.VMEM((seq, CH, LANES), BF16),
            pltpu.VMEM((seq, CH, LANES), BF16),
            pltpu.VMEM((seq, CH, LANES), BF16),
            pltpu.VMEM((seq, CH, LANES), BF16),
            pltpu.VMEM((d, LANES), BF16),
            pltpu.VMEM((2, nx, cw, LANES), BF16),
            pltpu.VMEM((2, nx, cw, LANES), BF16),
            pltpu.VMEM((nx, LANES, cw), BF16),
            pltpu.VMEM((nx, LANES, cw), BF16),
            pltpu.VMEM((LANES, d), BF16),
            pltpu.VMEM((LANES, d), F32),
            pltpu.VMEM((nz, CH, d), BF16),
            pltpu.VMEM((nz, CH, d), BF16),
            pltpu.VMEM((cw, d), F32),
            dma((4 * nx + 3,)),
            dma((2, 4, seq)),
            dma((2, 4, seq)),
            dma((nx,)),
            dma((nx,)),
            dma((2, nx)),
            dma((2, nx)),
            dma((2, 2)),
            dma((2, 2)),
            dma((2, 2)),
            dma((2, 2)),
            dma((nz,)),
            dma((nz,)),
        ],
        compiler_params=pltpu.CompilerParams(
            collective_id=0, has_side_effects=True, vmem_limit_bytes=60 * 1024 * 1024),
    )(resident[0], ids.reshape(1, LANES), sizes, amino, poly, gain, win[0], kernels[0], skips[0], wout[0],
      seeds[0], fk, fi, tw, g)
    return passed[None], grad[None]


SEQ = ("seq_0", "seq_1")


def build(mesh, ns, nx, nz):
    torus = Mesh(mesh.devices.reshape(ns, nx, nz), ("section", "seq_0", "seq_1"))
    placed = (
        P("section", SEQ, None),
        P(SEQ),
        P(),
        P(),
        P(),
        P("section", None),
        P("section", None, None),
        P("section", None, SEQ, None),
        P("section", None, SEQ),
        P("section", None, None),
        P("section", None, SEQ, None),
    )
    return jax.shard_map(
        lambda *args: local((ns, nx, nz), *args),
        mesh=torus,
        in_specs=placed,
        out_specs=(P("section", SEQ, None), P("section", SEQ, None)),
        check_vma=False,
    )


def solution(mesh):
    return build(mesh, mesh.shape["section"], 4, 8)
```

```python
import math

import jax
import jax.numpy as jnp
import numpy as np
from jax import lax
from jax.experimental import pallas as pl
from jax.experimental.pallas import tpu as pltpu
from jax.sharding import Mesh
from jax.sharding import PartitionSpec as P

MESH = pl.DeviceIdType.MESH
F32 = jnp.float32
BF16 = jnp.bfloat16
EPS = 1e-06
LANES = 128
CH = 32


def dft_tables(blocks):
    n = LANES * blocks
    a = np.arange(blocks)[None, :]
    k1 = np.arange(blocks)[:, None]
    first = 2.0 * math.pi * a * (k1 + 0.25) / blocks
    eye = np.eye(8)
    fwd = np.kron(np.concatenate([np.cos(first), -np.sin(first)], axis=0), eye)
    inv = np.kron(np.concatenate([np.cos(first).T, -np.sin(first).T], axis=1), eye)
    q = np.arange(LANES)[None, :]
    twist = np.repeat(2.0 * math.pi * q * (k1 + 0.25) / n, 8, axis=0)
    last = 2.0 * math.pi * (np.arange(LANES)[:, None] * q % LANES) / LANES
    c, s = np.cos(last), np.sin(last)
    g_fwd = np.block([[c, -s], [s, c]])
    g_inv = np.block([[c, s], [-s, c]])
    return (
        jnp.asarray(fwd, BF16),
        jnp.asarray(inv, BF16),
        jnp.asarray(np.stack([np.cos(twist), np.sin(twist)]), F32),
        jnp.asarray(np.stack([g_fwd, g_inv]), BF16),
    )


def dot(a, b):
    return lax.dot_general(a, b, (((1,), (0,)), ((), ())), preferred_element_type=F32)


def body(ns, nx, nz,
         x_hbm, ids_hbm, sizes_hbm, amino_hbm, poly_hbm, gain_hbm, win_hbm, h_hbm, skip_hbm, wout_hbm,
         seeds_hbm, fk_hbm, fi_hbm, tw_hbm, g_hbm,
         passed_ref, grad_ref,
         x_ref, ids_ref, sizes_ref, amino_ref, poly_ref, gain_ref, skip_ref, fk_ref, fi_ref, tw_ref, g_ref,
         win, wout, h, spec, sall, vg_send, vg_recv, m_send, m_recv, g2t, hyt, yall, hsend, hrecv,
         emb, tab, acc, part, rsend, rrecv,
         lsem, vg_s, vg_r, m_s, m_r, sh_s, sh_r, y_s, y_r, s_s, s_r, f_s, f_r, z_s, z_r):
    seq = nx * nz
    d = CH * seq
    cw = CH * nz
    hw = cw // 2
    rows = 8 * seq
    sec, x, z = lax.axis_index("section"), lax.axis_index("seq_0"), lax.axis_index("seq_1")
    me = x * nz + z
    left, right = lax.rem(x + nx - 1, nx), lax.rem(x + 1, nx)
    after, before = lax.rem(sec + 1, ns), lax.rem(sec + ns - 1, ns)

    copies = {}

    def fetch(name, src, dst):
        copies[name] = pltpu.make_async_copy(src, dst, lsem.at[len(copies)])
        copies[name].start()

    fetch("x", x_hbm, x_ref)
    fetch("gain", gain_hbm, gain_ref)
    for p in range(3):
        for j in range(nx):
            fetch(("win", p, j), win_hbm.at[:, pl.ds((p * nx + j) * cw, cw)], win.at[p, j])

    barrier = pltpu.get_barrier_semaphore()

    def greet(i, carry):
        peer = lax.rem(me + i, seq)
        pl.semaphore_signal(barrier, inc=1, device_id=(sec, peer // nz, lax.rem(peer, nz)), device_id_type=MESH)
        return carry

    pl.semaphore_signal(barrier, inc=1, device_id=(after, x, z), device_id_type=MESH)
    pl.semaphore_signal(barrier, inc=1, device_id=(before, x, z), device_id_type=MESH)
    lax.fori_loop(1, seq, greet, 0)

    fetch("fk", fk_hbm, fk_ref)
    fetch("tw", tw_hbm, tw_ref)
    fetch("g", g_hbm, g_ref)
    fetch("h", h_hbm, h)
    fetch("ids", ids_hbm, ids_ref)
    fetch("sizes", sizes_hbm, sizes_ref)
    fetch("amino", amino_hbm, amino_ref)
    fetch("poly", poly_hbm, poly_ref)
    fetch("skip", skip_hbm, skip_ref)
    fetch("fi", fi_hbm, fi_ref)
    for step in range(2):
        fetch(("seed", step), seeds_hbm.at[step], sall.at[step, x])
    for j in range(nx):
        fetch(("wout", j), wout_hbm.at[:, pl.ds(j * cw, cw)], wout.at[j])

    def far(i):
        half = (i + 1) // 2
        return nz // 2 + half * (1 - 2 * lax.rem(i, 2))

    orders = [o % nx for o in (2, 1, 3, 0)]

    def block_to(peer, src, dst, send_sem, recv_sem):
        pltpu.make_async_remote_copy(
            src_ref=src.at[peer], dst_ref=dst.at[me], send_sem=send_sem, recv_sem=recv_sem,
            device_id=(sec, peer // nz, lax.rem(peer, nz)), device_id_type=MESH).start()

    def send_column(o, src, dst, send_sem, recv_sem):
        xx = lax.rem(x + o, nx)

        def one(i, carry):
            block_to(xx * nz + lax.rem(z + far(i), nz), src, dst, send_sem, recv_sem)
            return carry

        lax.fori_loop(0, nz - 1, one, 0)
        if o:
            block_to(xx * nz + z, src, dst, send_sem, recv_sem)
        else:
            dst[me] = src[me]

    def wait_all(ref, sem):
        block = ref.at[pl.ds(0, seq - 1)]
        pltpu.make_async_copy(block, block, sem).wait()

    def send_vg(k, half, o):
        send_column(o, vg_send.at[half], vg_recv.at[half], vg_s.at[k, half], vg_r.at[k, half])

    def send_mixed(k, half):
        for o in orders:
            send_column(o, m_send.at[half], m_recv.at[half], m_s.at[k, half], m_r.at[k, half])

    def wait_vg(k, half):
        wait_all(vg_recv.at[half], vg_r.at[k, half])

    def wait_mixed(k, half):
        wait_all(m_recv.at[half], m_r.at[k, half])

    def wait_sent(k):
        for half in range(2):
            wait_all(vg_send.at[half], vg_s.at[k, half])
            wait_all(m_send.at[half], m_s.at[k, half])

    def along_x(ref, send_sem, recv_sem, direction):
        return pltpu.make_async_remote_copy(
            src_ref=ref, dst_ref=ref, send_sem=send_sem, recv_sem=recv_sem,
            device_id=(sec, (right, left)[direction], z), device_id_type=MESH)

    def seed_copy(step, w):
        return along_x(sall.at[step, x], s_s.at[step, w], s_r.at[step, w], w)

    def seed_arrival(step, w):
        return along_x(sall.at[step, (left, right)[w]], s_s.at[step, w], s_r.at[step, w], w)

    def forward_copy(step, w):
        return along_x(sall.at[step, (left, right)[w], pl.ds(64 * w, 64)], f_s.at[step, w], f_r.at[step, w], w)

    def forward_arrival(step, w):
        return along_x(sall.at[step, lax.rem(x + 2, nx), pl.ds(64 * w, 64)], f_s.at[step, w], f_r.at[step, w], w)

    def forward(xin):
        first = dot(fk_ref[...], xin)
        wc, ws = tw_ref[0], tw_ref[1]
        outs = []
        for k in range(2):
            re, im = first[:rows, LANES * k:LANES * k + LANES], first[rows:, LANES * k:LANES * k + LANES]
            turned = jnp.concatenate([re * wc + im * ws, im * wc - re * ws], axis=1).astype(BF16)
            outs.append(dot(turned, g_ref[0]))
        return outs

    def long_filter(xin, f, pair):
        wc, ws = tw_ref[0], tw_ref[1]
        cols = []
        for k, zz in enumerate(forward(xin)):
            s = spec[f, 2 * pair + k]
            zr, zi, hr, hi = zz[:, :LANES], zz[:, LANES:], s[:, :LANES], s[:, LANES:]
            prod = jnp.concatenate([zr * hr - zi * hi, zr * hi + zi * hr], axis=1).astype(BF16)
            back = dot(prod, g_ref[1])
            br, bi = back[:, :LANES], back[:, LANES:]
            cols.append(jnp.concatenate([br * wc - bi * ws, br * ws + bi * wc], axis=0).astype(BF16))
        return dot(fi_ref[...], jnp.concatenate(cols, axis=1))

    def rows_of(half, which):
        v = vg_recv[half, :, which].astype(F32)
        return jnp.concatenate([v[:, :8, :].reshape(rows, LANES), v[:, 8:, :].reshape(rows, LANES)], axis=1)

    def skip_tile(f, group):
        row = lax.broadcasted_iota(jnp.int32, (8, LANES), 0)
        out = jnp.zeros((8, LANES), F32)
        for r in range(8):
            out = jnp.where(row == r, skip_ref[f, 8 * group + r], out)
        return out

    def with_skip(y, f, pair, xin):
        gains = jnp.concatenate([skip_tile(f, 2 * pair), skip_tile(f, 2 * pair + 1)], axis=1)
        return y + (xin.reshape(seq, 8, 2 * LANES) * gains[None]).reshape(rows, 2 * LANES)

    def convolve(pair):
        v = rows_of(pair, 0)
        y = with_skip(long_filter(v.astype(BF16), 0, pair), 0, pair, v)
        gated = rows_of(pair, 1) * y
        y = with_skip(long_filter(gated.astype(BF16), 1, pair), 1, pair, gated)
        y = y.reshape(seq, 8, 2 * LANES)
        out = jnp.concatenate([y[:, :, :LANES], y[:, :, LANES:]], axis=1)
        m_send[pair] = out.astype(BF16)

    def filter_spectra(f, pair):
        scale = 1.0 / (LANES * seq)
        cols = []
        for k in range(2):
            lo = 16 * pair + 8 * k
            cols.append(jnp.concatenate(
                [h[f, lo:lo + 8, LANES * a:LANES * a + LANES] for a in range(seq)], axis=0))
        outs = forward(jnp.concatenate(cols, axis=1).astype(BF16))
        for k in range(2):
            spec[f, 2 * pair + k] = outs[k] * scale

    def embed():
        token = lax.broadcasted_iota(jnp.int32, (LANES, LANES), 0)
        pos = me * LANES + lax.broadcasted_iota(jnp.int32, (LANES, LANES), 1)
        chain = jnp.zeros((LANES, LANES), jnp.int32)
        end = jnp.int32(0)
        for j in range(7):
            end = end + sizes_ref[j]
            chain = chain + jnp.where(pos >= end, 1, 0)
        vocab = amino_ref.shape[0]
        ids = jnp.broadcast_to(ids_ref[...], (LANES, LANES))
        hot = jnp.where(token < vocab, jnp.where(token == ids, 1.0, 0.0), jnp.where(token - vocab == chain, 1.0, 0.0))
        tab[...] = jnp.zeros_like(tab)
        tab[:vocab] = amino_ref[...].astype(F32)
        tab[vocab:vocab + 8] = poly_ref[...].astype(F32)
        emb[...] = dot(hot.astype(F32).T.astype(BF16), tab[...].astype(BF16)).astype(BF16)

    per = cw // CH

    def project(p, xx, normed):
        chunk = dot(normed, win[p, xx]).T.astype(BF16).reshape(per, 2, 16, LANES)
        for half in range(2):
            vg_send[half, pl.ds(xx * per, per), p] = chunk[:, half]

    def project_gate(j, normed):
        chunk = dot(normed, win[2, j]).T.astype(BF16).reshape(per, 2, 16, LANES)
        for half in range(2):
            g2t[half, pl.ds(j * hw, hw)] = chunk[:, half].reshape(hw, LANES)

    def y_copy(step, half, xx, to):
        return pltpu.make_async_remote_copy(
            src_ref=hyt.at[step, half, xx], dst_ref=yall.at[step, half, x if to else xx],
            send_sem=y_s.at[step, half, xx], recv_sem=y_r.at[step, half, x if to else xx],
            device_id=(sec, xx, z), device_id_type=MESH)

    def make_hyena(k, half):
        hyena = m_recv[half].reshape(d // 2, LANES).astype(F32) * g2t[half].astype(F32)
        hyt[k, half] = hyena.astype(BF16).reshape(nx, hw, LANES)
        for o in orders:
            if o:
                y_copy(k, half, lax.rem(x + o, nx), True).start()
        yall[k, half, x] = hyt[k, half, x]
        return hyena.T.astype(BF16)

    def wait_y(step, half):
        for o in range(1, nx):
            y_copy(step, half, lax.rem(x + o, nx), False).wait_recv()

    def grad_of(step, half):
        y = jnp.concatenate([yall[step, half, j] for j in range(nx)], axis=1)
        half_d = d // 2
        for n in range(2):
            cols = slice(n * half_d, (n + 1) * half_d)
            s = jnp.concatenate([sall[step, j, :, cols] for j in range(nx)], axis=0)
            term = dot(y, s)
            if step == 0:
                part[half, :, cols] = term
            else:
                part[half, :, cols] = part[half, :, cols] + term

    def exit_rows(half, j):
        w = wout[j].reshape(seq, 2, 16, cw)
        return w[:, half].reshape(d // 2, cw)

    def half_exit(hyena_rows):
        for j in range(nx):
            acc[:, j * cw:(j + 1) * cw] = dot(hyena_rows, exit_rows(0, j))

    def normalize(values):
        return (values * lax.rsqrt(jnp.mean(values * values, axis=1, keepdims=True) + EPS) * gain_ref[...]).astype(BF16)

    def layer(k, normed):
        for o in orders:
            xx = lax.rem(x + o, nx)
            project(0, xx, normed)
            project(1, xx, normed)
            if k == 0 and o == orders[0]:
                pl.semaphore_wait(barrier, seq + 1)
            send_vg(k, 0, o)
        for o in orders:
            send_vg(k, 1, o)
        if k == 1:
            for step in range(2):
                for w in range(2):
                    seed_arrival(step, w).wait_recv()
                    forward_copy(step, w).start()
        else:
            for j in range(nx):
                copies["win", 2, j].wait()
        for j in range(nx):
            project_gate(j, normed)
        if k == 0:
            for name in ("h", "fk", "tw", "g", "fi", "skip", "ids", "sizes", "amino", "poly"):
                copies[name].wait()
            for pair in range(2):
                for f in range(2):
                    filter_spectra(f, pair)
            embed()
        for half in range(2):
            wait_vg(k, half)
            convolve(half)
            send_mixed(k, half)
        if k == 0:
            for step in range(2):
                copies["seed", step].wait()
                seed_copy(step, 0).start()
                seed_copy(step, 1).start()
            for j in range(nx):
                copies["wout", j].wait()
        else:
            for step in range(2):
                for w in range(2):
                    forward_arrival(step, w).wait_recv()
            for half in range(2):
                wait_y(0, half)
                grad_of(0, half)
        wait_mixed(k, 0)
        first_rows = make_hyena(k, 0)
        half_exit(first_rows)
        wait_mixed(k, 1)
        return make_hyena(k, 1)

    def shift_copy(j):
        return pltpu.make_async_remote_copy(
            src_ref=hsend.at[j], dst_ref=hrecv.at[j], send_sem=sh_s.at[j], recv_sem=sh_r.at[j],
            device_id=(after, x, z), device_id_type=MESH)

    def wait_shift():
        for j in range(nx):
            shift_copy(j).wait_recv()

    copies["x"].wait()
    copies["gain"].wait()
    first_normed = normalize(x_ref[...].astype(F32))
    for p in range(2):
        for j in range(nx):
            copies["win", p, j].wait()
    hyena_rows = layer(0, first_normed)
    for j in range(nx):
        cols = slice(j * cw, (j + 1) * cw)
        out = x_ref[:, cols].astype(F32) + (acc[:, cols] + dot(hyena_rows, exit_rows(1, j)))
        hsend[j] = out.astype(BF16)
        shift_copy(j).start()
    wait_sent(0)
    wait_shift()
    handed = jnp.concatenate([hrecv[j] for j in range(nx)], axis=1)
    head = lax.broadcast(sec, (LANES, d)) == 0
    second_in = jnp.where(head, emb[...].astype(F32), handed.astype(F32))
    emb[...] = second_in.astype(BF16)
    hyena_rows = layer(1, normalize(second_in))

    def z_copy(half, zz, to):
        return pltpu.make_async_remote_copy(
            src_ref=rsend.at[half, zz], dst_ref=rrecv.at[half, z if to else zz], send_sem=z_s.at[half, zz],
            recv_sem=z_r.at[half, z if to else zz], device_id=(sec, x, zz), device_id_type=MESH)

    def send_partials(half):
        rsend[half] = part[half].astype(BF16).reshape(nz, 16, d)

        def one(i, carry):
            z_copy(half, lax.rem(z + far(i), nz), True).start()
            return carry

        lax.fori_loop(0, nz - 1, one, 0)
        grad_ref[16 * half:16 * half + 16] = part[half, pl.ds(pl.multiple_of(z * 16, 16), 16), :]

    def add_partials(half):
        def one(i, carry):
            zz = lax.rem(z + i, nz)
            z_copy(half, zz, False).wait_recv()
            grad_ref[16 * half:16 * half + 16] = grad_ref[16 * half:16 * half + 16] + rrecv[half, zz].astype(F32)
            return carry

        lax.fori_loop(1, nz, one, 0)

    wait_y(1, 0)
    grad_of(1, 0)
    send_partials(0)
    for j in range(nx):
        cols = slice(j * cw, (j + 1) * cw)
        out = emb[:, cols].astype(F32) + (acc[:, cols] + dot(hyena_rows, exit_rows(1, j)))
        passed_ref[:, cols] = out.astype(BF16)
    wait_y(1, 1)
    grad_of(1, 1)
    send_partials(1)

    wait_sent(1)
    for j in range(nx):
        shift_copy(j).wait_send()
    for step in range(2):
        for w in range(2):
            seed_copy(step, w).wait_send()
            forward_copy(step, w).wait_send()
        for half in range(2):
            for o in range(1, nx):
                y_copy(step, half, lax.rem(x + o, nx), True).wait_send()
    add_partials(0)
    add_partials(1)

    def z_drain(i, carry):
        for half in range(2):
            z_copy(half, lax.rem(z + i, nz), True).wait_send()
        return carry

    lax.fori_loop(1, nz, z_drain, 0)


def local(shape, resident, ids, sizes, amino, poly, gain, win, kernels, skips, wout, seeds):
    ns, nx, nz = shape
    seq = nx * nz
    d = CH * seq
    cw = CH * nz
    hw = cw // 2
    fk, fi, tw, g = dft_tables(seq)
    vmem = pl.BlockSpec(memory_space=pltpu.VMEM)
    hbm = pl.BlockSpec(memory_space=pl.ANY)
    dma = pltpu.SemaphoreType.DMA
    operands = (resident[0], ids.reshape(1, LANES), sizes, amino, poly, gain, win[0], kernels[0], skips[0], wout[0],
                seeds[0], fk, fi, tw, g)

    def like(i, space=pltpu.VMEM):
        return space(operands[i].shape, operands[i].dtype)

    passed, grad = pl.pallas_call(
        lambda *refs: body(ns, nx, nz, *refs),
        out_shape=(jax.ShapeDtypeStruct((LANES, d), BF16), jax.ShapeDtypeStruct((CH, d), F32)),
        in_specs=[hbm] * len(operands),
        out_specs=(vmem, vmem),
        scratch_shapes=[
            like(0), like(1), like(2, pltpu.SMEM), like(3), like(4), like(5), like(8, pltpu.SMEM),
            like(11), like(12), like(13), like(14),
            pltpu.VMEM((3, nx, d, cw), BF16),
            pltpu.VMEM((nx, d, cw), BF16),
            pltpu.VMEM((2, CH, LANES * seq), F32),
            pltpu.VMEM((2, 4, 8 * seq, 2 * LANES), F32),
            pltpu.VMEM((2, nx, LANES, d), BF16),
            pltpu.VMEM((2, seq, 2, 16, LANES), BF16),
            pltpu.VMEM((2, seq, 2, 16, LANES), BF16),
            pltpu.VMEM((2, seq, 16, LANES), BF16),
            pltpu.VMEM((2, seq, 16, LANES), BF16),
            pltpu.VMEM((2, d // 2, LANES), BF16),
            pltpu.VMEM((2, 2, nx, hw, LANES), BF16),
            pltpu.VMEM((2, 2, nx, hw, LANES), BF16),
            pltpu.VMEM((nx, LANES, cw), BF16),
            pltpu.VMEM((nx, LANES, cw), BF16),
            pltpu.VMEM((LANES, d), BF16),
            pltpu.VMEM((LANES, d), F32),
            pltpu.VMEM((LANES, d), F32),
            pltpu.VMEM((2, hw, d), F32),
            pltpu.VMEM((2, nz, 16, d), BF16),
            pltpu.VMEM((2, nz, 16, d), BF16),
            dma((4 * nx + 14,)),
            dma((2, 2)),
            dma((2, 2)),
            dma((2, 2)),
            dma((2, 2)),
            dma((nx,)),
            dma((nx,)),
            dma((2, 2, nx)),
            dma((2, 2, nx)),
            dma((2, 2)),
            dma((2, 2)),
            dma((2, 2)),
            dma((2, 2)),
            dma((2, nz)),
            dma((2, nz)),
        ],
        compiler_params=pltpu.CompilerParams(
            collective_id=0, has_side_effects=True, vmem_limit_bytes=60 * 1024 * 1024),
    )(*operands)
    return passed[None], grad[None]


SEQ = ("seq_0", "seq_1")


def build(mesh, ns, nx, nz):
    torus = Mesh(mesh.devices.reshape(ns, nx, nz), ("section", "seq_0", "seq_1"))
    placed = (
        P("section", SEQ, None),
        P(SEQ),
        P(),
        P(),
        P(),
        P("section", None),
        P("section", None, None),
        P("section", None, SEQ, None),
        P("section", None, SEQ),
        P("section", None, None),
        P("section", None, SEQ, None),
    )
    return jax.shard_map(
        lambda *args: local((ns, nx, nz), *args),
        mesh=torus,
        in_specs=placed,
        out_specs=(P("section", SEQ, None), P("section", SEQ, None)),
        check_vma=False,
    )


def solution(mesh):
    return build(mesh, mesh.shape["section"], 4, 8)
```

```python
import math

import jax
import jax.numpy as jnp
import numpy as np
from jax import lax
from jax.experimental import pallas as pl
from jax.experimental.pallas import tpu as pltpu
from jax.sharding import Mesh
from jax.sharding import PartitionSpec as P

MESH = pl.DeviceIdType.MESH
F32 = jnp.float32
BF16 = jnp.bfloat16
EPS = 1e-06
LANES = 128
CH = 32


def dft_tables(blocks):
    n = LANES * blocks
    a = np.arange(blocks)[None, :]
    k1 = np.arange(blocks)[:, None]
    first = 2.0 * math.pi * a * (k1 + 0.25) / blocks
    eye = np.eye(8)
    fwd = np.kron(np.concatenate([np.cos(first), -np.sin(first)], axis=0), eye)
    inv = np.kron(np.concatenate([np.cos(first).T, -np.sin(first).T], axis=1), eye)
    q = np.arange(LANES)[None, :]
    twist = np.repeat(2.0 * math.pi * q * (k1 + 0.25) / n, 8, axis=0)
    last = 2.0 * math.pi * (np.arange(LANES)[:, None] * q % LANES) / LANES
    c, s = np.cos(last), np.sin(last)
    g_fwd = np.block([[c, -s], [s, c]])
    g_inv = np.block([[c, s], [-s, c]])
    return (
        jnp.asarray(fwd, BF16),
        jnp.asarray(inv, BF16),
        jnp.asarray(np.stack([np.cos(twist), np.sin(twist)]), F32),
        jnp.asarray(np.stack([g_fwd, g_inv]), BF16),
    )


def dot(a, b):
    return lax.dot_general(a, b, (((1,), (0,)), ((), ())), preferred_element_type=F32)


def body(ns, nx, nz,
         x_hbm, ids_hbm, sizes_hbm, amino_hbm, poly_hbm, gain_hbm, win_hbm, h_hbm, skip_hbm, wout_hbm,
         seeds_hbm, fk_hbm, fi_hbm, tw_hbm, g_hbm,
         passed_ref, grad_ref,
         x_ref, ids_ref, sizes_ref, amino_ref, poly_ref, gain_ref, skip_ref, fk_ref, fi_ref, tw_ref, g_ref,
         win, wout, h, spec, sall, vg_send, vg_recv, m_send, m_recv, m1_send, m1_recv, g2t, g2x, hyt, yall, hsend, hrecv,
         emb, tab, acc, part, rsend, rrecv,
         lsem, vg_s, vg_r, m_s, m_r, m1_s, m1_r, m2_s, m2_r, g2_s, g2_r, sh_s, sh_r, y_s, y_r, s_s, s_r, f_s, f_r, z_s, z_r):
    seq = nx * nz
    d = CH * seq
    cw = CH * nz
    hw = cw // 2
    rows = 8 * seq
    sec, x, z = lax.axis_index("section"), lax.axis_index("seq_0"), lax.axis_index("seq_1")
    me = x * nz + z
    left, right = lax.rem(x + nx - 1, nx), lax.rem(x + 1, nx)
    after, before = lax.rem(sec + 1, ns), lax.rem(sec + ns - 1, ns)

    copies = {}

    def fetch(name, src, dst):
        copies[name] = pltpu.make_async_copy(src, dst, lsem.at[len(copies)])
        copies[name].start()

    fetch("x", x_hbm, x_ref)
    fetch("gain", gain_hbm, gain_ref)
    for p in range(3):
        for j in range(nx):
            fetch(("win", p, j), win_hbm.at[:, pl.ds((p * nx + j) * cw, cw)], win.at[p, j])

    barrier = pltpu.get_barrier_semaphore()

    def greet(i, carry):
        peer = lax.rem(me + i, seq)
        pl.semaphore_signal(barrier, inc=1, device_id=(sec, peer // nz, lax.rem(peer, nz)), device_id_type=MESH)
        return carry

    pl.semaphore_signal(barrier, inc=1, device_id=(after, x, z), device_id_type=MESH)
    pl.semaphore_signal(barrier, inc=1, device_id=(before, x, z), device_id_type=MESH)
    lax.fori_loop(1, seq, greet, 0)

    fetch("fk", fk_hbm, fk_ref)
    fetch("tw", tw_hbm, tw_ref)
    fetch("g", g_hbm, g_ref)
    fetch("h", h_hbm, h)
    fetch("ids", ids_hbm, ids_ref)
    fetch("sizes", sizes_hbm, sizes_ref)
    fetch("amino", amino_hbm, amino_ref)
    fetch("poly", poly_hbm, poly_ref)
    fetch("skip", skip_hbm, skip_ref)
    fetch("fi", fi_hbm, fi_ref)
    for step in range(2):
        fetch(("seed", step), seeds_hbm.at[step], sall.at[step, x])
    for j in range(nx):
        fetch(("wout", j), wout_hbm.at[:, pl.ds(j * cw, cw)], wout.at[j])

    def far(i):
        half = (i + 1) // 2
        return nz // 2 + half * (1 - 2 * lax.rem(i, 2))

    orders = [o % nx for o in (2, 1, 3, 0)]

    def block_to(peer, src, dst, send_sem, recv_sem):
        pltpu.make_async_remote_copy(
            src_ref=src.at[peer], dst_ref=dst.at[me], send_sem=send_sem, recv_sem=recv_sem,
            device_id=(sec, peer // nz, lax.rem(peer, nz)), device_id_type=MESH).start()

    def send_column(o, src, dst, send_sem, recv_sem):
        xx = lax.rem(x + o, nx)

        def one(i, carry):
            block_to(xx * nz + lax.rem(z + far(i), nz), src, dst, send_sem, recv_sem)
            return carry

        lax.fori_loop(0, nz - 1, one, 0)
        if o:
            block_to(xx * nz + z, src, dst, send_sem, recv_sem)
        else:
            dst[me] = src[me]

    def wait_all(ref, sem):
        block = ref.at[pl.ds(0, ref.shape[0] - 1)]
        pltpu.make_async_copy(block, block, sem).wait()

    def send_vg(k, half, o):
        send_column(o, vg_send.at[half], vg_recv.at[half], vg_s.at[k, half], vg_r.at[k, half])

    def send_mixed(k, half):
        if k == 0:
            for o in orders:
                send_column(o, m_send.at[half], m_recv.at[half], m_s.at[half], m_r.at[half])
        else:
            send_along_z(half)

    def send_along_z(half):
        def one(i, carry):
            zz = lax.rem(z + far(i), nz)
            pltpu.make_async_remote_copy(
                src_ref=m1_send.at[half, zz], dst_ref=m1_recv.at[half, z], send_sem=m1_s.at[half],
                recv_sem=m1_r.at[half], device_id=(sec, x, zz), device_id_type=MESH).start()
            return carry

        lax.fori_loop(0, nz - 1, one, 0)
        m1_recv[half, z] = m1_send[half, z]

    def wait_along_z(half):
        wait_all(m1_recv.at[half], m1_r.at[half])

    def on_copy(half, xx, to):
        return pltpu.make_async_remote_copy(
            src_ref=m1_recv.at[half, :, xx], dst_ref=m_recv.at[half, pl.ds((x if to else xx) * nz, nz)],
            send_sem=m2_s.at[half, xx], recv_sem=m2_r.at[half, x if to else xx],
            device_id=(sec, xx, z), device_id_type=MESH)

    def send_on(half):
        for o in orders:
            if o:
                on_copy(half, lax.rem(x + o, nx), True).start()
        m_recv[half, pl.ds(x * nz, nz)] = m1_recv[half, :, x]

    def gate_copy(xx, to):
        return pltpu.make_async_remote_copy(
            src_ref=g2t.at[xx], dst_ref=g2x.at[x if to else xx], send_sem=g2_s.at[xx],
            recv_sem=g2_r.at[x if to else xx], device_id=(sec, xx, z), device_id_type=MESH)

    def send_gates():
        for o in orders:
            if o:
                gate_copy(lax.rem(x + o, nx), True).start()
        g2x[x] = g2t[x]

    def wait_gates():
        for o in range(1, nx):
            gate_copy(lax.rem(x + o, nx), False).wait_recv()

    def hyena_along_x(half):
        for j in range(nx):
            y = m1_recv[half, :, j].reshape(hw, LANES).astype(F32) * g2x[j, half].astype(F32)
            yall[1, half, j] = y.astype(BF16)

    def wait_vg(k, half):
        wait_all(vg_recv.at[half], vg_r.at[k, half])

    def wait_mixed(k, half):
        if k == 0:
            wait_all(m_recv.at[half], m_r.at[half])
        else:
            for o in range(1, nx):
                on_copy(half, lax.rem(x + o, nx), False).wait_recv()

    def wait_sent(k):
        for half in range(2):
            wait_all(vg_send.at[half], vg_s.at[k, half])
            if k == 0:
                wait_all(m_send.at[half], m_s.at[half])
            else:
                wait_all(m1_send.at[half], m1_s.at[half])

    def along_x(ref, send_sem, recv_sem, direction):
        return pltpu.make_async_remote_copy(
            src_ref=ref, dst_ref=ref, send_sem=send_sem, recv_sem=recv_sem,
            device_id=(sec, (right, left)[direction], z), device_id_type=MESH)

    def seed_copy(step, w):
        return along_x(sall.at[step, x], s_s.at[step, w], s_r.at[step, w], w)

    def seed_arrival(step, w):
        return along_x(sall.at[step, (left, right)[w]], s_s.at[step, w], s_r.at[step, w], w)

    def forward_copy(step, w):
        return along_x(sall.at[step, (left, right)[w], pl.ds(64 * w, 64)], f_s.at[step, w], f_r.at[step, w], w)

    def forward_arrival(step, w):
        return along_x(sall.at[step, lax.rem(x + 2, nx), pl.ds(64 * w, 64)], f_s.at[step, w], f_r.at[step, w], w)

    def forward(xin):
        first = dot(fk_ref[...], xin)
        wc, ws = tw_ref[0], tw_ref[1]
        outs = []
        for k in range(2):
            re, im = first[:rows, LANES * k:LANES * k + LANES], first[rows:, LANES * k:LANES * k + LANES]
            turned = jnp.concatenate([re * wc + im * ws, im * wc - re * ws], axis=1).astype(BF16)
            outs.append(dot(turned, g_ref[0]))
        return outs

    def long_filter(xin, f, pair):
        wc, ws = tw_ref[0], tw_ref[1]
        cols = []
        for k, zz in enumerate(forward(xin)):
            s = spec[f, 2 * pair + k]
            zr, zi, hr, hi = zz[:, :LANES], zz[:, LANES:], s[:, :LANES], s[:, LANES:]
            prod = jnp.concatenate([zr * hr - zi * hi, zr * hi + zi * hr], axis=1).astype(BF16)
            back = dot(prod, g_ref[1])
            br, bi = back[:, :LANES], back[:, LANES:]
            cols.append(jnp.concatenate([br * wc - bi * ws, br * ws + bi * wc], axis=0).astype(BF16))
        return dot(fi_ref[...], jnp.concatenate(cols, axis=1))

    def rows_of(half, which):
        v = vg_recv[half, :, which].astype(F32)
        return jnp.concatenate([v[:, :8, :].reshape(rows, LANES), v[:, 8:, :].reshape(rows, LANES)], axis=1)

    def skip_tile(f, group):
        row = lax.broadcasted_iota(jnp.int32, (8, LANES), 0)
        out = jnp.zeros((8, LANES), F32)
        for r in range(8):
            out = jnp.where(row == r, skip_ref[f, 8 * group + r], out)
        return out

    def with_skip(y, f, pair, xin):
        gains = jnp.concatenate([skip_tile(f, 2 * pair), skip_tile(f, 2 * pair + 1)], axis=1)
        return y + (xin.reshape(seq, 8, 2 * LANES) * gains[None]).reshape(rows, 2 * LANES)

    def convolve(k, pair):
        v = rows_of(pair, 0)
        y = with_skip(long_filter(v.astype(BF16), 0, pair), 0, pair, v)
        gated = rows_of(pair, 1) * y
        y = with_skip(long_filter(gated.astype(BF16), 1, pair), 1, pair, gated)
        y = y.reshape(seq, 8, 2 * LANES)
        out = jnp.concatenate([y[:, :, :LANES], y[:, :, LANES:]], axis=1)
        out = out.astype(BF16)
        if k == 0:
            m_send[pair] = out
        else:
            for j in range(nx):
                m1_send[pair, :, j] = out[j * nz:(j + 1) * nz]

    def filter_spectra(f, pair):
        scale = 1.0 / (LANES * seq)
        cols = []
        for k in range(2):
            lo = 16 * pair + 8 * k
            cols.append(jnp.concatenate(
                [h[f, lo:lo + 8, LANES * a:LANES * a + LANES] for a in range(seq)], axis=0))
        outs = forward(jnp.concatenate(cols, axis=1).astype(BF16))
        for k in range(2):
            spec[f, 2 * pair + k] = outs[k] * scale

    def embed():
        token = lax.broadcasted_iota(jnp.int32, (LANES, LANES), 0)
        pos = me * LANES + lax.broadcasted_iota(jnp.int32, (LANES, LANES), 1)
        chain = jnp.zeros((LANES, LANES), jnp.int32)
        end = jnp.int32(0)
        for j in range(7):
            end = end + sizes_ref[j]
            chain = chain + jnp.where(pos >= end, 1, 0)
        vocab = amino_ref.shape[0]
        ids = jnp.broadcast_to(ids_ref[...], (LANES, LANES))
        hot = jnp.where(token < vocab, jnp.where(token == ids, 1.0, 0.0), jnp.where(token - vocab == chain, 1.0, 0.0))
        tab[...] = jnp.zeros_like(tab)
        tab[:vocab] = amino_ref[...].astype(F32)
        tab[vocab:vocab + 8] = poly_ref[...].astype(F32)
        emb[...] = dot(hot.astype(F32).T.astype(BF16), tab[...].astype(BF16)).astype(BF16)

    per = cw // CH

    def project(p, xx, normed):
        chunk = dot(normed, win[p, xx]).T.astype(BF16).reshape(per, 2, 16, LANES)
        for half in range(2):
            vg_send[half, pl.ds(xx * per, per), p] = chunk[:, half]

    def project_gate(j, normed):
        chunk = dot(normed, win[2, j]).T.astype(BF16).reshape(per, 2, 16, LANES)
        for half in range(2):
            g2t[j, half] = chunk[:, half].reshape(hw, LANES)

    def y_copy(half, xx, to):
        return pltpu.make_async_remote_copy(
            src_ref=hyt.at[half, xx], dst_ref=yall.at[0, half, x if to else xx],
            send_sem=y_s.at[half, xx], recv_sem=y_r.at[half, x if to else xx],
            device_id=(sec, xx, z), device_id_type=MESH)

    def make_hyena(k, half):
        hyena = m_recv[half].reshape(d // 2, LANES).astype(F32) * g2t[:, half].reshape(d // 2, LANES).astype(F32)
        if k == 0:
            hyt[half] = hyena.astype(BF16).reshape(nx, hw, LANES)
            for o in orders:
                if o:
                    y_copy(half, lax.rem(x + o, nx), True).start()
            yall[0, half, x] = hyt[half, x]
        return hyena.T.astype(BF16)

    def wait_y(half):
        for o in range(1, nx):
            y_copy(half, lax.rem(x + o, nx), False).wait_recv()

    def grad_of(step, half):
        y = jnp.concatenate([yall[step, half, j] for j in range(nx)], axis=1)
        half_d = d // 2
        for n in range(2):
            cols = slice(n * half_d, (n + 1) * half_d)
            s = jnp.concatenate([sall[step, j, :, cols] for j in range(nx)], axis=0)
            term = dot(y, s)
            if step == 0:
                part[half, :, cols] = term
            else:
                part[half, :, cols] = part[half, :, cols] + term

    def exit_rows(half, j):
        w = wout[j].reshape(seq, 2, 16, cw)
        return w[:, half].reshape(d // 2, cw)

    def half_exit(hyena_rows):
        for j in range(nx):
            acc[:, j * cw:(j + 1) * cw] = dot(hyena_rows, exit_rows(0, j))

    def normalize(values):
        return (values * lax.rsqrt(jnp.mean(values * values, axis=1, keepdims=True) + EPS) * gain_ref[...]).astype(BF16)

    def z_copy(half, zz, to):
        return pltpu.make_async_remote_copy(
            src_ref=rsend.at[half, zz], dst_ref=rrecv.at[half, z if to else zz], send_sem=z_s.at[half, zz],
            recv_sem=z_r.at[half, z if to else zz], device_id=(sec, x, zz), device_id_type=MESH)

    def send_partials(half):
        rsend[half] = part[half].astype(BF16).reshape(nz, 16, d)

        def one(i, carry):
            z_copy(half, lax.rem(z + far(i), nz), True).start()
            return carry

        lax.fori_loop(0, nz - 1, one, 0)
        grad_ref[16 * half:16 * half + 16] = part[half, pl.ds(pl.multiple_of(z * 16, 16), 16), :]

    def add_partials(half):
        def one(i, carry):
            zz = lax.rem(z + i, nz)
            z_copy(half, zz, False).wait_recv()
            grad_ref[16 * half:16 * half + 16] = grad_ref[16 * half:16 * half + 16] + rrecv[half, zz].astype(F32)
            return carry

        lax.fori_loop(1, nz, one, 0)

    def send_seeds(step):
        copies["seed", step].wait()
        seed_copy(step, 0).start()
        seed_copy(step, 1).start()

    def forward_seeds(step):
        for w in range(2):
            seed_arrival(step, w).wait_recv()
            forward_copy(step, w).start()

    def layer(k, normed):
        for o in orders:
            xx = lax.rem(x + o, nx)
            project(0, xx, normed)
            project(1, xx, normed)
            if k == 0 and o == orders[0]:
                pl.semaphore_wait(barrier, seq + 1)
            send_vg(k, 0, o)
        for o in orders:
            send_vg(k, 1, o)
        if k == 0:
            send_seeds(0)
            for j in range(nx):
                copies["win", 2, j].wait()
        for j in range(nx):
            project_gate(j, normed)
        if k == 1:
            send_gates()
            forward_seeds(1)
        if k == 0:
            for name in ("h", "fk", "tw", "g", "fi", "skip", "ids", "sizes", "amino", "poly"):
                copies[name].wait()
            for pair in range(2):
                for f in range(2):
                    filter_spectra(f, pair)
            embed()
        for half in range(2):
            wait_vg(k, half)
            convolve(k, half)
            send_mixed(k, half)
        if k == 0:
            send_seeds(1)
            for j in range(nx):
                copies["wout", j].wait()
        else:
            for step in range(2):
                for w in range(2):
                    forward_arrival(step, w).wait_recv()
            for half in range(2):
                wait_y(half)
                grad_of(0, half)
            wait_gates()
            for half in range(2):
                wait_along_z(half)
                send_on(half)
                hyena_along_x(half)
                grad_of(1, half)
                send_partials(half)
        wait_mixed(k, 0)
        first_rows = make_hyena(k, 0)
        half_exit(first_rows)
        wait_mixed(k, 1)
        second_rows = make_hyena(k, 1)
        if k == 0:
            forward_seeds(0)
        return second_rows

    def shift_copy(j):
        return pltpu.make_async_remote_copy(
            src_ref=hsend.at[j], dst_ref=hrecv.at[j], send_sem=sh_s.at[j], recv_sem=sh_r.at[j],
            device_id=(after, x, z), device_id_type=MESH)

    def wait_shift():
        for j in range(nx):
            shift_copy(j).wait_recv()

    copies["x"].wait()
    copies["gain"].wait()
    first_normed = normalize(x_ref[...].astype(F32))
    for p in range(2):
        for j in range(nx):
            copies["win", p, j].wait()
    hyena_rows = layer(0, first_normed)
    for j in range(nx):
        cols = slice(j * cw, (j + 1) * cw)
        out = x_ref[:, cols].astype(F32) + (acc[:, cols] + dot(hyena_rows, exit_rows(1, j)))
        hsend[j] = out.astype(BF16)
        shift_copy(j).start()
    wait_sent(0)
    wait_shift()
    handed = jnp.concatenate([hrecv[j] for j in range(nx)], axis=1)
    head = lax.broadcast(sec, (LANES, d)) == 0
    second_in = jnp.where(head, emb[...].astype(F32), handed.astype(F32))
    emb[...] = second_in.astype(BF16)
    hyena_rows = layer(1, normalize(second_in))

    for j in range(nx):
        cols = slice(j * cw, (j + 1) * cw)
        out = emb[:, cols].astype(F32) + (acc[:, cols] + dot(hyena_rows, exit_rows(1, j)))
        passed_ref[:, cols] = out.astype(BF16)
    wait_sent(1)
    for j in range(nx):
        shift_copy(j).wait_send()
    for step in range(2):
        for w in range(2):
            seed_copy(step, w).wait_send()
            forward_copy(step, w).wait_send()
    for o in range(1, nx):
        xx = lax.rem(x + o, nx)
        gate_copy(xx, True).wait_send()
        for half in range(2):
            y_copy(half, xx, True).wait_send()
            on_copy(half, xx, True).wait_send()
    add_partials(0)
    add_partials(1)

    def z_drain(i, carry):
        for half in range(2):
            z_copy(half, lax.rem(z + i, nz), True).wait_send()
        return carry

    lax.fori_loop(1, nz, z_drain, 0)


def local(shape, resident, ids, sizes, amino, poly, gain, win, kernels, skips, wout, seeds):
    ns, nx, nz = shape
    seq = nx * nz
    d = CH * seq
    cw = CH * nz
    hw = cw // 2
    fk, fi, tw, g = dft_tables(seq)
    vmem = pl.BlockSpec(memory_space=pltpu.VMEM)
    hbm = pl.BlockSpec(memory_space=pl.ANY)
    dma = pltpu.SemaphoreType.DMA
    operands = (resident[0], ids.reshape(1, LANES), sizes, amino, poly, gain, win[0], kernels[0], skips[0], wout[0],
                seeds[0], fk, fi, tw, g)

    def like(i, space=pltpu.VMEM):
        return space(operands[i].shape, operands[i].dtype)

    passed, grad = pl.pallas_call(
        lambda *refs: body(ns, nx, nz, *refs),
        out_shape=(pltpu.VMEM((LANES, d), BF16), pltpu.VMEM((CH, d), F32)),
        in_specs=[hbm] * len(operands),
        out_specs=(vmem, vmem),
        scratch_shapes=[
            like(0), like(1), like(2, pltpu.SMEM), like(3), like(4), like(5), like(8, pltpu.SMEM),
            like(11), like(12), like(13), like(14),
            pltpu.VMEM((3, nx, d, cw), BF16),
            pltpu.VMEM((nx, d, cw), BF16),
            pltpu.VMEM((2, CH, LANES * seq), F32),
            pltpu.VMEM((2, 4, 8 * seq, 2 * LANES), F32),
            pltpu.VMEM((2, nx, LANES, d), BF16),
            pltpu.VMEM((2, seq, 2, 16, LANES), BF16),
            pltpu.VMEM((2, seq, 2, 16, LANES), BF16),
            pltpu.VMEM((2, seq, 16, LANES), BF16),
            pltpu.VMEM((2, seq, 16, LANES), BF16),
            pltpu.VMEM((2, nz, nx, 16, LANES), BF16),
            pltpu.VMEM((2, nz, nx, 16, LANES), BF16),
            pltpu.VMEM((nx, 2, hw, LANES), BF16),
            pltpu.VMEM((nx, 2, hw, LANES), BF16),
            pltpu.VMEM((2, nx, hw, LANES), BF16),
            pltpu.VMEM((2, 2, nx, hw, LANES), BF16),
            pltpu.VMEM((nx, LANES, cw), BF16),
            pltpu.VMEM((nx, LANES, cw), BF16),
            pltpu.VMEM((LANES, d), BF16),
            pltpu.VMEM((LANES, d), F32),
            pltpu.VMEM((LANES, d), F32),
            pltpu.VMEM((2, hw, d), F32),
            pltpu.VMEM((2, nz, 16, d), BF16),
            pltpu.VMEM((2, nz, 16, d), BF16),
            dma((4 * nx + 14,)),
            dma((2, 2)),
            dma((2, 2)),
            dma((2,)),
            dma((2,)),
            dma((2,)),
            dma((2,)),
            dma((2, nx)),
            dma((2, nx)),
            dma((nx,)),
            dma((nx,)),
            dma((nx,)),
            dma((nx,)),
            dma((2, nx)),
            dma((2, nx)),
            dma((2, 2)),
            dma((2, 2)),
            dma((2, 2)),
            dma((2, 2)),
            dma((2, nz)),
            dma((2, nz)),
        ],
        compiler_params=pltpu.CompilerParams(
            collective_id=0, has_side_effects=True, vmem_limit_bytes=66600000),
    )(*operands)
    return passed[None], grad[None]


SEQ = ("seq_0", "seq_1")


def build(mesh, ns, nx, nz):
    torus = Mesh(mesh.devices.reshape(ns, nx, nz), ("section", "seq_0", "seq_1"))
    placed = (
        P("section", SEQ, None),
        P(SEQ),
        P(),
        P(),
        P(),
        P("section", None),
        P("section", None, None),
        P("section", None, SEQ, None),
        P("section", None, SEQ),
        P("section", None, None),
        P("section", None, SEQ, None),
    )
    return jax.shard_map(
        lambda *args: local((ns, nx, nz), *args),
        mesh=torus,
        in_specs=placed,
        out_specs=(P("section", SEQ, None), P("section", SEQ, None)),
        check_vma=False,
    )


def solution(mesh):
    return build(mesh, mesh.shape["section"], 4, 8)
```

```python
import math

import jax
import jax.numpy as jnp
import numpy as np
from jax import lax
from jax.experimental import pallas as pl
from jax.experimental.pallas import tpu as pltpu
from jax.sharding import Mesh
from jax.sharding import PartitionSpec as P

MESH = pl.DeviceIdType.MESH
F32 = jnp.float32
BF16 = jnp.bfloat16
EPS = 1e-06
LANES = 128
CH = 32


def dft_tables(blocks):
    n = LANES * blocks
    a = np.arange(blocks)[None, :]
    k1 = np.arange(blocks)[:, None]
    first = 2.0 * math.pi * a * (k1 + 0.25) / blocks
    eye = np.eye(8)
    fwd = np.kron(np.concatenate([np.cos(first), -np.sin(first)], axis=0), eye)
    inv = np.kron(np.concatenate([np.cos(first).T, -np.sin(first).T], axis=1), eye)
    q = np.arange(LANES)[None, :]
    twist = np.repeat(2.0 * math.pi * q * (k1 + 0.25) / n, 8, axis=0)
    last = 2.0 * math.pi * (np.arange(LANES)[:, None] * q % LANES) / LANES
    c, s = np.cos(last), np.sin(last)
    g_fwd = np.block([[c, -s], [s, c]])
    g_inv = np.block([[c, s], [-s, c]])
    return (
        jnp.asarray(fwd, BF16),
        jnp.asarray(inv, BF16),
        jnp.asarray(np.stack([np.cos(twist), np.sin(twist)]), F32),
        jnp.asarray(np.stack([g_fwd, g_inv]), BF16),
    )


def dot(a, b):
    return lax.dot_general(a, b, (((1,), (0,)), ((), ())), preferred_element_type=F32)


def body(ns, nx, nz,
         x_hbm, ids_hbm, sizes_hbm, amino_hbm, poly_hbm, gain_hbm, win_hbm, h_hbm, skip_hbm, wout_hbm,
         seeds_hbm, fk_hbm, fi_hbm, tw_hbm, g_hbm,
         passed_ref, grad_ref,
         x_ref, ids_ref, sizes_ref, amino_ref, poly_ref, gain_ref, skip_ref, fk_ref, fi_ref, tw_ref, g_ref,
         win, wout, h, spec, sall, vg_send, vg_recv, w_send, w_recv, m_send, m_recv, m1_send, m1_recv, g2t, g2x, hyt, yall, hsend, hrecv,
         emb, tab, acc, part, rsend, rrecv,
         lsem, vg_s, vg_r, w_s, w_r, m_s, m_r, m1_s, m1_r, m2_s, m2_r, g2_s, g2_r, sh_s, sh_r, y_s, y_r, s_s, s_r, f_s, f_r, z_s, z_r):
    seq = nx * nz
    d = CH * seq
    cw = CH * nz
    hw = cw // 2
    rows = 8 * seq
    sec, x, z = lax.axis_index("section"), lax.axis_index("seq_0"), lax.axis_index("seq_1")
    me = x * nz + z
    left, right = lax.rem(x + nx - 1, nx), lax.rem(x + 1, nx)
    after, before = lax.rem(sec + 1, ns), lax.rem(sec + ns - 1, ns)

    copies = {}

    def fetch(name, src, dst):
        copies[name] = pltpu.make_async_copy(src, dst, lsem.at[len(copies)])
        copies[name].start()

    def far(i):
        half = (i + 1) // 2
        return nz // 2 + half * (1 - 2 * lax.rem(i, 2))

    orders = [o % nx for o in (2, 1, 3, 0)]
    columns = [lax.rem(x + o, nx) for o in orders]

    barrier = pltpu.get_barrier_semaphore()

    def greet(dev):
        pl.semaphore_signal(barrier, inc=1, device_id=dev, device_id_type=MESH)

    fetch("x", x_hbm, x_ref)
    for xx, o in zip(columns, orders):
        def one(i, carry, xx=xx):
            greet((sec, xx, lax.rem(z + far(i), nz)))
            return carry

        lax.fori_loop(0, nz - 1, one, 0)
        if o:
            greet((sec, xx, z))
    greet((after, x, z))
    greet((before, x, z))

    fetch("gain", gain_hbm, gain_ref)
    for xx, o in zip(columns, orders):
        for p in range(2):
            fetch(("win", p, o), win_hbm.at[:, pl.ds(pl.multiple_of((p * nx + xx) * cw, cw), cw)], win.at[p, xx])
    for j in range(nx):
        fetch(("win", 2, j), win_hbm.at[:, pl.ds((2 * nx + j) * cw, cw)], win.at[2, j])
    fetch("fk", fk_hbm, fk_ref)
    fetch("tw", tw_hbm, tw_ref)
    fetch("g", g_hbm, g_ref)
    fetch("h", h_hbm, h)
    fetch("ids", ids_hbm, ids_ref)
    fetch("sizes", sizes_hbm, sizes_ref)
    fetch("amino", amino_hbm, amino_ref)
    fetch("poly", poly_hbm, poly_ref)
    fetch("skip", skip_hbm, skip_ref)
    fetch("fi", fi_hbm, fi_ref)
    for step in range(2):
        fetch(("seed", step), seeds_hbm.at[step], sall.at[step, x])
    for j in range(nx):
        fetch(("wout", j), wout_hbm.at[:, pl.ds(j * cw, cw)], wout.at[j])

    def block_to(peer, src, dst, send_sem, recv_sem):
        pltpu.make_async_remote_copy(
            src_ref=src.at[peer], dst_ref=dst.at[me], send_sem=send_sem, recv_sem=recv_sem,
            device_id=(sec, peer // nz, lax.rem(peer, nz)), device_id_type=MESH).start()

    def send_column(o, src, dst, send_sem, recv_sem):
        xx = lax.rem(x + o, nx)

        def one(i, carry):
            block_to(xx * nz + lax.rem(z + far(i), nz), src, dst, send_sem, recv_sem)
            return carry

        lax.fori_loop(0, nz - 1, one, 0)
        if o:
            block_to(xx * nz + z, src, dst, send_sem, recv_sem)
        else:
            dst[me] = src[me]

    def wait_all(ref, sem):
        block = ref.at[pl.ds(0, ref.shape[0] - 1)]
        pltpu.make_async_copy(block, block, sem).wait()

    def send_vg(k, o):
        send_column(o, vg_send, vg_recv, vg_s.at[k], vg_r.at[k])

    def send_w(k, p):
        for o in orders:
            send_column(o, w_send.at[p], w_recv.at[p], w_s.at[k, p], w_r.at[k, p])

    def send_mixed(k, half):
        if k == 0:
            for o in orders:
                send_column(o, m_send.at[half], m_recv.at[half], m_s.at[half], m_r.at[half])
        else:
            send_along_z(half)

    def send_along_z(half):
        def one(i, carry):
            zz = lax.rem(z + far(i), nz)
            pltpu.make_async_remote_copy(
                src_ref=m1_send.at[half, zz], dst_ref=m1_recv.at[half, z], send_sem=m1_s.at[half],
                recv_sem=m1_r.at[half], device_id=(sec, x, zz), device_id_type=MESH).start()
            return carry

        lax.fori_loop(0, nz - 1, one, 0)
        m1_recv[half, z] = m1_send[half, z]

    def wait_along_z(half):
        wait_all(m1_recv.at[half], m1_r.at[half])

    def on_copy(half, xx, to):
        return pltpu.make_async_remote_copy(
            src_ref=m1_recv.at[half, :, xx], dst_ref=m_recv.at[half, pl.ds((x if to else xx) * nz, nz)],
            send_sem=m2_s.at[half, xx], recv_sem=m2_r.at[half, x if to else xx],
            device_id=(sec, xx, z), device_id_type=MESH)

    def send_on(half):
        for o in orders:
            if o:
                on_copy(half, lax.rem(x + o, nx), True).start()
        m_recv[half, pl.ds(x * nz, nz)] = m1_recv[half, :, x]

    def gate_copy(xx, to):
        return pltpu.make_async_remote_copy(
            src_ref=g2t.at[xx], dst_ref=g2x.at[x if to else xx], send_sem=g2_s.at[xx],
            recv_sem=g2_r.at[x if to else xx], device_id=(sec, xx, z), device_id_type=MESH)

    def send_gates():
        for o in orders:
            if o:
                gate_copy(lax.rem(x + o, nx), True).start()
        g2x[x] = g2t[x]

    def wait_gates():
        for o in range(1, nx):
            gate_copy(lax.rem(x + o, nx), False).wait_recv()

    def hyena_along_x(half):
        for j in range(nx):
            y = m1_recv[half, :, j].reshape(hw, LANES).astype(F32) * g2x[j, half].astype(F32)
            yall[1, half, j] = y.astype(BF16)

    def wait_vg(k):
        wait_all(vg_recv, vg_r.at[k])

    def wait_w(k, p):
        wait_all(w_recv.at[p], w_r.at[k, p])

    def wait_mixed(k, half):
        if k == 0:
            wait_all(m_recv.at[half], m_r.at[half])
        else:
            for o in range(1, nx):
                on_copy(half, lax.rem(x + o, nx), False).wait_recv()

    def wait_sent(k):
        wait_all(vg_send, vg_s.at[k])
        for half in range(2):
            wait_all(w_send.at[half], w_s.at[k, half])
            if k == 0:
                wait_all(m_send.at[half], m_s.at[half])
            else:
                wait_all(m1_send.at[half], m1_s.at[half])

    def along_x(ref, send_sem, recv_sem, direction):
        return pltpu.make_async_remote_copy(
            src_ref=ref, dst_ref=ref, send_sem=send_sem, recv_sem=recv_sem,
            device_id=(sec, (right, left)[direction], z), device_id_type=MESH)

    def seed_copy(step, w):
        return along_x(sall.at[step, x], s_s.at[step, w], s_r.at[step, w], w)

    def seed_arrival(step, w):
        return along_x(sall.at[step, (left, right)[w]], s_s.at[step, w], s_r.at[step, w], w)

    def forward_copy(step, w):
        return along_x(sall.at[step, (left, right)[w], pl.ds(64 * w, 64)], f_s.at[step, w], f_r.at[step, w], w)

    def forward_arrival(step, w):
        return along_x(sall.at[step, lax.rem(x + 2, nx), pl.ds(64 * w, 64)], f_s.at[step, w], f_r.at[step, w], w)

    def forward(xin):
        first = dot(fk_ref[...], xin)
        wc, ws = tw_ref[0], tw_ref[1]
        outs = []
        for k in range(2):
            re, im = first[:rows, LANES * k:LANES * k + LANES], first[rows:, LANES * k:LANES * k + LANES]
            turned = jnp.concatenate([re * wc + im * ws, im * wc - re * ws], axis=1).astype(BF16)
            outs.append(dot(turned, g_ref[0]))
        return outs

    def long_filter(xin, f, pair):
        wc, ws = tw_ref[0], tw_ref[1]
        cols = []
        for k, zz in enumerate(forward(xin)):
            s = spec[f, 2 * pair + k]
            zr, zi, hr, hi = zz[:, :LANES], zz[:, LANES:], s[:, :LANES], s[:, LANES:]
            prod = jnp.concatenate([zr * hr - zi * hi, zr * hi + zi * hr], axis=1).astype(BF16)
            back = dot(prod, g_ref[1])
            br, bi = back[:, :LANES], back[:, LANES:]
            cols.append(jnp.concatenate([br * wc - bi * ws, br * ws + bi * wc], axis=0).astype(BF16))
        return dot(fi_ref[...], jnp.concatenate(cols, axis=1))

    def rows_of(half, which):
        v = (w_recv[which] if half else vg_recv[:, which]).astype(F32)
        return jnp.concatenate([v[:, :8, :].reshape(rows, LANES), v[:, 8:, :].reshape(rows, LANES)], axis=1)

    def skip_tile(f, group):
        row = lax.broadcasted_iota(jnp.int32, (8, LANES), 0)
        out = jnp.zeros((8, LANES), F32)
        for r in range(8):
            out = jnp.where(row == r, skip_ref[f, 8 * group + r], out)
        return out

    def with_skip(y, f, pair, xin):
        gains = jnp.concatenate([skip_tile(f, 2 * pair), skip_tile(f, 2 * pair + 1)], axis=1)
        return y + (xin.reshape(seq, 8, 2 * LANES) * gains[None]).reshape(rows, 2 * LANES)

    def convolve(k, pair):
        if pair:
            wait_w(k, 0)
        else:
            wait_vg(k)
        v = rows_of(pair, 0)
        y = with_skip(long_filter(v.astype(BF16), 0, pair), 0, pair, v)
        if pair:
            wait_w(k, 1)
        gated = rows_of(pair, 1) * y
        y = with_skip(long_filter(gated.astype(BF16), 1, pair), 1, pair, gated)
        y = y.reshape(seq, 8, 2 * LANES)
        out = jnp.concatenate([y[:, :, :LANES], y[:, :, LANES:]], axis=1)
        out = out.astype(BF16)
        if k == 0:
            m_send[pair] = out
        else:
            for j in range(nx):
                m1_send[pair, :, j] = out[j * nz:(j + 1) * nz]

    def filter_spectra(f, pair):
        scale = 1.0 / (LANES * seq)
        cols = []
        for k in range(2):
            lo = 16 * pair + 8 * k
            cols.append(jnp.concatenate(
                [h[f, lo:lo + 8, LANES * a:LANES * a + LANES] for a in range(seq)], axis=0))
        outs = forward(jnp.concatenate(cols, axis=1).astype(BF16))
        for k in range(2):
            spec[f, 2 * pair + k] = outs[k] * scale

    def embed():
        token = lax.broadcasted_iota(jnp.int32, (LANES, LANES), 0)
        pos = me * LANES + lax.broadcasted_iota(jnp.int32, (LANES, LANES), 1)
        chain = jnp.zeros((LANES, LANES), jnp.int32)
        end = jnp.int32(0)
        for j in range(7):
            end = end + sizes_ref[j]
            chain = chain + jnp.where(pos >= end, 1, 0)
        vocab = amino_ref.shape[0]
        ids = jnp.broadcast_to(ids_ref[...], (LANES, LANES))
        hot = jnp.where(token < vocab, jnp.where(token == ids, 1.0, 0.0), jnp.where(token - vocab == chain, 1.0, 0.0))
        tab[...] = jnp.zeros_like(tab)
        tab[:vocab] = amino_ref[...].astype(F32)
        tab[vocab:vocab + 8] = poly_ref[...].astype(F32)
        emb[...] = dot(hot.astype(F32).T.astype(BF16), tab[...].astype(BF16)).astype(BF16)

    per = cw // CH

    def project(p, xx, normed):
        chunk = dot(normed, win[p, xx]).T.astype(BF16).reshape(per, 2, 16, LANES)
        vg_send[pl.ds(xx * per, per), p] = chunk[:, 0]
        w_send[p, pl.ds(xx * per, per)] = chunk[:, 1]

    def project_gate(j, normed):
        chunk = dot(normed, win[2, j]).T.astype(BF16).reshape(per, 2, 16, LANES)
        for half in range(2):
            g2t[j, half] = chunk[:, half].reshape(hw, LANES)

    def y_copy(half, xx, to):
        return pltpu.make_async_remote_copy(
            src_ref=hyt.at[half, xx], dst_ref=yall.at[0, half, x if to else xx],
            send_sem=y_s.at[half, xx], recv_sem=y_r.at[half, x if to else xx],
            device_id=(sec, xx, z), device_id_type=MESH)

    def make_hyena(k, half):
        hyena = m_recv[half].reshape(d // 2, LANES).astype(F32) * g2t[:, half].reshape(d // 2, LANES).astype(F32)
        if k == 0:
            hyt[half] = hyena.astype(BF16).reshape(nx, hw, LANES)
            for o in orders:
                if o:
                    y_copy(half, lax.rem(x + o, nx), True).start()
            yall[0, half, x] = hyt[half, x]
        return hyena.T.astype(BF16)

    def wait_y(half):
        for o in range(1, nx):
            y_copy(half, lax.rem(x + o, nx), False).wait_recv()

    def grad_of(step, half):
        y = jnp.concatenate([yall[step, half, j] for j in range(nx)], axis=1)
        half_d = d // 2
        for n in range(2):
            cols = slice(n * half_d, (n + 1) * half_d)
            s = jnp.concatenate([sall[step, j, :, cols] for j in range(nx)], axis=0)
            term = dot(y, s)
            if step == 0:
                part[half, :, cols] = term
            else:
                part[half, :, cols] = part[half, :, cols] + term

    def exit_rows(half, j):
        w = wout[j].reshape(seq, 2, 16, cw)
        return w[:, half].reshape(d // 2, cw)

    def half_exit(hyena_rows):
        for j in range(nx):
            acc[:, j * cw:(j + 1) * cw] = dot(hyena_rows, exit_rows(0, j))

    def normalize(values):
        return (values * lax.rsqrt(jnp.mean(values * values, axis=1, keepdims=True) + EPS) * gain_ref[...]).astype(BF16)

    def z_copy(half, zz, to):
        return pltpu.make_async_remote_copy(
            src_ref=rsend.at[half, zz], dst_ref=rrecv.at[half, z if to else zz], send_sem=z_s.at[half, zz],
            recv_sem=z_r.at[half, z if to else zz], device_id=(sec, x, zz), device_id_type=MESH)

    def send_partials(half):
        rsend[half] = part[half].astype(BF16).reshape(nz, 16, d)

        def one(i, carry):
            z_copy(half, lax.rem(z + far(i), nz), True).start()
            return carry

        lax.fori_loop(0, nz - 1, one, 0)
        grad_ref[16 * half:16 * half + 16] = part[half, pl.ds(pl.multiple_of(z * 16, 16), 16), :]

    def add_partials(half):
        def one(i, carry):
            zz = lax.rem(z + i, nz)
            z_copy(half, zz, False).wait_recv()
            grad_ref[16 * half:16 * half + 16] = grad_ref[16 * half:16 * half + 16] + rrecv[half, zz].astype(F32)
            return carry

        lax.fori_loop(1, nz, one, 0)

    def send_seeds(step):
        copies["seed", step].wait()
        seed_copy(step, 0).start()
        seed_copy(step, 1).start()

    def wait_seeds(step):
        for w in range(2):
            forward_arrival(step, w).wait_recv()

    def forward_seeds(step):
        for w in range(2):
            seed_arrival(step, w).wait_recv()
            forward_copy(step, w).start()

    def layer(k, normed):
        for xx, o in zip(columns, orders):
            for p in range(2):
                if k == 0:
                    copies["win", p, o].wait()
                project(p, xx, normed)
            if k == 0 and o == orders[0]:
                pl.semaphore_wait(barrier, seq + 1)
            send_vg(k, o)
        for p in range(2):
            send_w(k, p)
        if k == 0:
            send_seeds(0)
            for j in range(nx):
                copies["win", 2, j].wait()
        for j in range(nx):
            project_gate(j, normed)
        if k == 1:
            send_gates()
            forward_seeds(0)
        if k == 0:
            for name in ("h", "fk", "tw", "g", "fi", "skip", "ids", "sizes", "amino", "poly"):
                copies[name].wait()
            for pair in range(2):
                for f in range(2):
                    filter_spectra(f, pair)
            embed()
        for half in range(2):
            convolve(k, half)
            send_mixed(k, half)
            if k == 1 and half == 0:
                forward_seeds(1)
        if k == 0:
            send_seeds(1)
            for j in range(nx):
                copies["wout", j].wait()
        else:
            wait_seeds(0)
            wait_y(0)
            grad_of(0, 0)
            wait_gates()
            for half in range(2):
                wait_along_z(half)
                send_on(half)
                hyena_along_x(half)
                if half == 0:
                    wait_seeds(1)
                grad_of(1, half)
                send_partials(half)
                if half == 0:
                    wait_y(1)
                    grad_of(0, 1)
        wait_mixed(k, 0)
        first_rows = make_hyena(k, 0)
        half_exit(first_rows)
        wait_mixed(k, 1)
        second_rows = make_hyena(k, 1)
        return second_rows

    def shift_copy(j):
        return pltpu.make_async_remote_copy(
            src_ref=hsend.at[j], dst_ref=hrecv.at[j], send_sem=sh_s.at[j], recv_sem=sh_r.at[j],
            device_id=(after, x, z), device_id_type=MESH)

    def start_shift(j):
        @pl.when(sec < ns - 1)
        def _():
            shift_copy(j).start()

    def wait_shift():
        @pl.when(sec > 0)
        def _():
            for j in range(nx):
                shift_copy(j).wait_recv()
            emb[...] = jnp.concatenate([hrecv[j] for j in range(nx)], axis=1)

    copies["x"].wait()
    copies["gain"].wait()
    first_normed = normalize(x_ref[...].astype(F32))
    hyena_rows = layer(0, first_normed)
    for j in range(0, nx, 2):
        cols = slice(j * cw, (j + 2) * cw)
        w = jnp.concatenate([exit_rows(1, j), exit_rows(1, j + 1)], axis=1)
        out = (x_ref[:, cols].astype(F32) + (acc[:, cols] + dot(hyena_rows, w))).astype(BF16)
        for i in range(2):
            hsend[j + i] = out[:, i * cw:(i + 1) * cw]
            start_shift(j + i)
    wait_sent(0)
    wait_shift()
    hyena_rows = layer(1, normalize(emb[...].astype(F32)))

    for j in range(nx):
        cols = slice(j * cw, (j + 1) * cw)
        out = emb[:, cols].astype(F32) + (acc[:, cols] + dot(hyena_rows, exit_rows(1, j)))
        passed_ref[:, cols] = out.astype(BF16)
    wait_sent(1)
    @pl.when(sec < ns - 1)
    def _():
        for j in range(nx):
            shift_copy(j).wait_send()

    for step in range(2):
        for w in range(2):
            seed_copy(step, w).wait_send()
            forward_copy(step, w).wait_send()
    for o in range(1, nx):
        xx = lax.rem(x + o, nx)
        gate_copy(xx, True).wait_send()
        for half in range(2):
            y_copy(half, xx, True).wait_send()
            on_copy(half, xx, True).wait_send()
    add_partials(0)
    add_partials(1)

    def z_drain(i, carry):
        for half in range(2):
            z_copy(half, lax.rem(z + i, nz), True).wait_send()
        return carry

    lax.fori_loop(1, nz, z_drain, 0)


def local(shape, resident, ids, sizes, amino, poly, gain, win, kernels, skips, wout, seeds):
    ns, nx, nz = shape
    seq = nx * nz
    d = CH * seq
    cw = CH * nz
    hw = cw // 2
    fk, fi, tw, g = dft_tables(seq)
    vmem = pl.BlockSpec(memory_space=pltpu.VMEM)
    hbm = pl.BlockSpec(memory_space=pl.ANY)
    dma = pltpu.SemaphoreType.DMA
    operands = (resident[0], ids.reshape(1, LANES), sizes, amino, poly, gain, win[0], kernels[0], skips[0], wout[0],
                seeds[0], fk, fi, tw, g)

    def like(i, space=pltpu.VMEM):
        return space(operands[i].shape, operands[i].dtype)

    passed, grad = pl.pallas_call(
        lambda *refs: body(ns, nx, nz, *refs),
        out_shape=(pltpu.VMEM((LANES, d), BF16), pltpu.VMEM((CH, d), F32)),
        in_specs=[hbm] * len(operands),
        out_specs=(vmem, vmem),
        scratch_shapes=[
            like(0), like(1), like(2, pltpu.SMEM), like(3), like(4), like(5), like(8, pltpu.SMEM),
            like(11), like(12), like(13), like(14),
            pltpu.VMEM((3, nx, d, cw), BF16),
            pltpu.VMEM((nx, d, cw), BF16),
            pltpu.VMEM((2, CH, LANES * seq), F32),
            pltpu.VMEM((2, 4, 8 * seq, 2 * LANES), F32),
            pltpu.VMEM((2, nx, LANES, d), BF16),
            pltpu.VMEM((seq, 2, 16, LANES), BF16),
            pltpu.VMEM((seq, 2, 16, LANES), BF16),
            pltpu.VMEM((2, seq, 16, LANES), BF16),
            pltpu.VMEM((2, seq, 16, LANES), BF16),
            pltpu.VMEM((2, seq, 16, LANES), BF16),
            pltpu.VMEM((2, seq, 16, LANES), BF16),
            pltpu.VMEM((2, nz, nx, 16, LANES), BF16),
            pltpu.VMEM((2, nz, nx, 16, LANES), BF16),
            pltpu.VMEM((nx, 2, hw, LANES), BF16),
            pltpu.VMEM((nx, 2, hw, LANES), BF16),
            pltpu.VMEM((2, nx, hw, LANES), BF16),
            pltpu.VMEM((2, 2, nx, hw, LANES), BF16),
            pltpu.VMEM((nx, LANES, cw), BF16),
            pltpu.VMEM((nx, LANES, cw), BF16),
            pltpu.VMEM((LANES, d), BF16),
            pltpu.VMEM((LANES, d), F32),
            pltpu.VMEM((LANES, d), F32),
            pltpu.VMEM((2, hw, d), F32),
            pltpu.VMEM((2, nz, 16, d), BF16),
            pltpu.VMEM((2, nz, 16, d), BF16),
            dma((4 * nx + 14,)),
            dma((2,)),
            dma((2,)),
            dma((2, 2)),
            dma((2, 2)),
            dma((2,)),
            dma((2,)),
            dma((2,)),
            dma((2,)),
            dma((2, nx)),
            dma((2, nx)),
            dma((nx,)),
            dma((nx,)),
            dma((nx,)),
            dma((nx,)),
            dma((2, nx)),
            dma((2, nx)),
            dma((2, 2)),
            dma((2, 2)),
            dma((2, 2)),
            dma((2, 2)),
            dma((2, nz)),
            dma((2, nz)),
        ],
        compiler_params=pltpu.CompilerParams(
            collective_id=0, has_side_effects=True, vmem_limit_bytes=66600000),
    )(*operands)

    def write(passed_ref, grad_ref, passed_out, grad_out, sems):
        copies = [pltpu.make_async_copy(passed_ref, passed_out.at[0], sems.at[0]),
                  pltpu.make_async_copy(grad_ref, grad_out.at[0], sems.at[1])]
        for c in copies:
            c.start()
        for c in copies:
            c.wait()

    return pl.pallas_call(
        write,
        out_shape=(jax.ShapeDtypeStruct((1, LANES, d), BF16), jax.ShapeDtypeStruct((1, CH, d), F32)),
        in_specs=[vmem, vmem],
        out_specs=(hbm, hbm),
        scratch_shapes=[dma((2,))],
    )(*(pltpu.with_memory_space_constraint(t, pltpu.VMEM) for t in (passed, grad)))


SEQ = ("seq_0", "seq_1")


def build(mesh, ns, nx, nz):
    torus = Mesh(mesh.devices.reshape(ns, nx, nz), ("section", "seq_0", "seq_1"))
    placed = (
        P("section", SEQ, None),
        P(SEQ),
        P(),
        P(),
        P(),
        P("section", None),
        P("section", None, None),
        P("section", None, SEQ, None),
        P("section", None, SEQ),
        P("section", None, None),
        P("section", None, SEQ, None),
    )
    return jax.shard_map(
        lambda *args: local((ns, nx, nz), *args),
        mesh=torus,
        in_specs=placed,
        out_specs=(P("section", SEQ, None), P("section", SEQ, None)),
        check_vma=False,
    )


def solution(mesh):
    return build(mesh, mesh.shape["section"], 4, 8)
```

```python
import math

import jax
import jax.numpy as jnp
import numpy as np
from jax import lax
from jax.experimental import pallas as pl
from jax.experimental.pallas import tpu as pltpu
from jax.sharding import Mesh
from jax.sharding import PartitionSpec as P

MESH = pl.DeviceIdType.MESH
F32 = jnp.float32
BF16 = jnp.bfloat16
EPS = 1e-06
LANES = 128
CH = 32


def dft_tables(blocks):
    n = LANES * blocks
    a = np.arange(blocks)[None, :]
    k1 = np.arange(blocks)[:, None]
    first = 2.0 * math.pi * a * (k1 + 0.25) / blocks
    eye = np.eye(8)
    fwd = np.kron(np.concatenate([np.cos(first), -np.sin(first)], axis=0), eye)
    inv = np.kron(np.concatenate([np.cos(first).T, -np.sin(first).T], axis=1), eye)
    q = np.arange(LANES)[None, :]
    twist = np.repeat(2.0 * math.pi * q * (k1 + 0.25) / n, 8, axis=0)
    last = 2.0 * math.pi * (np.arange(LANES)[:, None] * q % LANES) / LANES
    c, s = np.cos(last), np.sin(last)
    g_fwd = np.block([[c, -s], [s, c]])
    g_inv = np.block([[c, s], [-s, c]])
    return (
        jnp.asarray(fwd, BF16),
        jnp.asarray(inv, BF16),
        jnp.asarray(np.stack([np.cos(twist), np.sin(twist)]), F32),
        jnp.asarray(np.stack([g_fwd, g_inv]), BF16),
    )


def dot(a, b):
    return lax.dot_general(a, b, (((1,), (0,)), ((), ())), preferred_element_type=F32)


def body(ns, nx, nz,
         x_hbm, ids_hbm, sizes_hbm, amino_hbm, poly_hbm, gain_hbm, win_hbm, h_hbm, skip_hbm, wout_hbm,
         seeds_hbm, fk_hbm, fi_hbm, tw_hbm, g_hbm,
         passed_ref, grad_ref,
         x_ref, ids_ref, sizes_ref, amino_ref, poly_ref, gain_ref, skip_ref, fk_ref, fi_ref, tw_ref, g_ref,
         win, wout, h, spec, sall, vg_send, vg_recv, w_send, w_recv, m_send, m_recv, m1_send, m1_recv, g2t, g2x, hyt, yall, hsend, hrecv,
         emb, tab, acc, part, rsend, rrecv,
         lsem, vg_s, vg_r, w_s, w_r, m_s, m_r, m1_s, m1_r, m2_s, m2_r, g2_s, g2_r, sh_s, sh_r, y_s, y_r, s_s, s_r, f_s, f_r, z_s, z_r):
    seq = nx * nz
    d = CH * seq
    cw = CH * nz
    hw = cw // 2
    rows = 8 * seq
    sec, x, z = lax.axis_index("section"), lax.axis_index("seq_0"), lax.axis_index("seq_1")
    me = x * nz + z
    left, right = lax.rem(x + nx - 1, nx), lax.rem(x + 1, nx)
    after, before = lax.rem(sec + 1, ns), lax.rem(sec + ns - 1, ns)

    copies = {}

    def fetch(name, src, dst):
        copies[name] = pltpu.make_async_copy(src, dst, lsem.at[len(copies)])
        copies[name].start()

    def far(i):
        half = (i + 1) // 2
        return nz // 2 + half * (1 - 2 * lax.rem(i, 2))

    orders = [o % nx for o in (2, 1, 3, 0)]
    columns = [lax.rem(x + o, nx) for o in orders]

    barrier = pltpu.get_barrier_semaphore()

    def greet(dev):
        pl.semaphore_signal(barrier, inc=1, device_id=dev, device_id_type=MESH)

    fetch("x", x_hbm, x_ref)
    for xx, o in zip(columns, orders):
        def one(i, carry, xx=xx):
            greet((sec, xx, lax.rem(z + far(i), nz)))
            return carry

        lax.fori_loop(0, nz - 1, one, 0)
        if o:
            greet((sec, xx, z))
    greet((after, x, z))
    greet((before, x, z))

    fetch("gain", gain_hbm, gain_ref)
    for xx, o in zip(columns, orders):
        for p in range(2):
            fetch(("win", p, o), win_hbm.at[:, pl.ds(pl.multiple_of((p * nx + xx) * cw, cw), cw)], win.at[p, xx])
    for j in range(nx):
        fetch(("win", 2, j), win_hbm.at[:, pl.ds((2 * nx + j) * cw, cw)], win.at[2, j])
    fetch("fk", fk_hbm, fk_ref)
    fetch("tw", tw_hbm, tw_ref)
    fetch("g", g_hbm, g_ref)
    fetch("h", h_hbm, h)
    fetch("ids", ids_hbm, ids_ref)
    fetch("sizes", sizes_hbm, sizes_ref)
    fetch("amino", amino_hbm, amino_ref)
    fetch("poly", poly_hbm, poly_ref)
    fetch("skip", skip_hbm, skip_ref)
    fetch("fi", fi_hbm, fi_ref)
    for step in range(2):
        fetch(("seed", step), seeds_hbm.at[step], sall.at[step, x])
    for j in range(nx):
        fetch(("wout", j), wout_hbm.at[:, pl.ds(j * cw, cw)], wout.at[j])

    def block_to(peer, src, dst, send_sem, recv_sem):
        pltpu.make_async_remote_copy(
            src_ref=src.at[peer], dst_ref=dst.at[me], send_sem=send_sem, recv_sem=recv_sem,
            device_id=(sec, peer // nz, lax.rem(peer, nz)), device_id_type=MESH).start()

    def send_column(o, src, dst, send_sem, recv_sem):
        xx = lax.rem(x + o, nx)

        def one(i, carry):
            block_to(xx * nz + lax.rem(z + far(i), nz), src, dst, send_sem, recv_sem)
            return carry

        lax.fori_loop(0, nz - 1, one, 0)
        if o:
            block_to(xx * nz + z, src, dst, send_sem, recv_sem)
        else:
            dst[me] = src[me]

    def wait_all(ref, sem):
        block = ref.at[pl.ds(0, ref.shape[0] - 1)]
        pltpu.make_async_copy(block, block, sem).wait()

    def send_vg(k, o):
        send_column(o, vg_send, vg_recv, vg_s.at[k], vg_r.at[k])

    def send_w(k, p):
        for o in orders:
            send_column(o, w_send.at[p], w_recv.at[p], w_s.at[k, p], w_r.at[k, p])

    def send_mixed(k, half):
        if k == 0:
            for o in orders:
                send_column(o, m_send.at[half], m_recv.at[half], m_s.at[half], m_r.at[half])
        else:
            send_along_z(half)

    def send_along_z(half):
        def one(i, carry):
            zz = lax.rem(z + far(i), nz)
            pltpu.make_async_remote_copy(
                src_ref=m1_send.at[half, zz], dst_ref=m1_recv.at[half, z], send_sem=m1_s.at[half],
                recv_sem=m1_r.at[half], device_id=(sec, x, zz), device_id_type=MESH).start()
            return carry

        lax.fori_loop(0, nz - 1, one, 0)
        m1_recv[half, z] = m1_send[half, z]

    def wait_along_z(half):
        wait_all(m1_recv.at[half], m1_r.at[half])

    def on_copy(half, xx, to):
        return pltpu.make_async_remote_copy(
            src_ref=m1_recv.at[half, :, xx], dst_ref=m_recv.at[half, pl.ds((x if to else xx) * nz, nz)],
            send_sem=m2_s.at[half, xx], recv_sem=m2_r.at[half, x if to else xx],
            device_id=(sec, xx, z), device_id_type=MESH)

    def send_on(half):
        for o in orders:
            if o:
                on_copy(half, lax.rem(x + o, nx), True).start()
        m_recv[half, pl.ds(x * nz, nz)] = m1_recv[half, :, x]

    def gate_copy(xx, to):
        return pltpu.make_async_remote_copy(
            src_ref=g2t.at[xx], dst_ref=g2x.at[x if to else xx], send_sem=g2_s.at[xx],
            recv_sem=g2_r.at[x if to else xx], device_id=(sec, xx, z), device_id_type=MESH)

    def send_gates():
        for o in orders:
            if o:
                gate_copy(lax.rem(x + o, nx), True).start()
        g2x[x] = g2t[x]

    def wait_gates():
        for o in range(1, nx):
            gate_copy(lax.rem(x + o, nx), False).wait_recv()

    def hyena_along_x(half):
        for j in range(nx):
            y = m1_recv[half, :, j].reshape(hw, LANES).astype(F32) * g2x[j, half].astype(F32)
            yall[1, half, j] = y.astype(BF16)

    def wait_vg(k):
        wait_all(vg_recv, vg_r.at[k])

    def wait_w(k, p):
        wait_all(w_recv.at[p], w_r.at[k, p])

    def wait_mixed(k, half):
        if k == 0:
            wait_all(m_recv.at[half], m_r.at[half])
        else:
            for o in range(1, nx):
                on_copy(half, lax.rem(x + o, nx), False).wait_recv()

    def wait_sent(k):
        wait_all(vg_send, vg_s.at[k])
        for half in range(2):
            wait_all(w_send.at[half], w_s.at[k, half])
            if k == 0:
                wait_all(m_send.at[half], m_s.at[half])
            else:
                wait_all(m1_send.at[half], m1_s.at[half])

    def along_x(ref, send_sem, recv_sem, direction):
        return pltpu.make_async_remote_copy(
            src_ref=ref, dst_ref=ref, send_sem=send_sem, recv_sem=recv_sem,
            device_id=(sec, (right, left)[direction], z), device_id_type=MESH)

    def seed_copy(step, w):
        return along_x(sall.at[step, x], s_s.at[step, w], s_r.at[step, w], w)

    def seed_arrival(step, w):
        return along_x(sall.at[step, (left, right)[w]], s_s.at[step, w], s_r.at[step, w], w)

    def forward_copy(step, w):
        return along_x(sall.at[step, (left, right)[w], pl.ds(64 * w, 64)], f_s.at[step, w], f_r.at[step, w], w)

    def forward_arrival(step, w):
        return along_x(sall.at[step, lax.rem(x + 2, nx), pl.ds(64 * w, 64)], f_s.at[step, w], f_r.at[step, w], w)

    def forward(xin):
        first = dot(fk_ref[...], xin)
        wc, ws = tw_ref[0], tw_ref[1]
        outs = []
        for k in range(2):
            re, im = first[:rows, LANES * k:LANES * k + LANES], first[rows:, LANES * k:LANES * k + LANES]
            turned = jnp.concatenate([re * wc + im * ws, im * wc - re * ws], axis=1).astype(BF16)
            outs.append(dot(turned, g_ref[0]))
        return outs

    def long_filter(xin, f, pair):
        wc, ws = tw_ref[0], tw_ref[1]
        cols = []
        for k, zz in enumerate(forward(xin)):
            s = spec[f, 2 * pair + k]
            zr, zi, hr, hi = zz[:, :LANES], zz[:, LANES:], s[:, :LANES], s[:, LANES:]
            prod = jnp.concatenate([zr * hr - zi * hi, zr * hi + zi * hr], axis=1).astype(BF16)
            back = dot(prod, g_ref[1])
            br, bi = back[:, :LANES], back[:, LANES:]
            cols.append(jnp.concatenate([br * wc - bi * ws, br * ws + bi * wc], axis=0).astype(BF16))
        return dot(fi_ref[...], jnp.concatenate(cols, axis=1))

    def rows_of(half, which):
        v = (w_recv[which] if half else vg_recv[:, which]).astype(F32)
        return jnp.concatenate([v[:, :8, :].reshape(rows, LANES), v[:, 8:, :].reshape(rows, LANES)], axis=1)

    def skip_tile(f, group):
        row = lax.broadcasted_iota(jnp.int32, (8, LANES), 0)
        out = jnp.zeros((8, LANES), F32)
        for r in range(8):
            out = jnp.where(row == r, skip_ref[f, 8 * group + r], out)
        return out

    def with_skip(y, f, pair, xin):
        gains = jnp.concatenate([skip_tile(f, 2 * pair), skip_tile(f, 2 * pair + 1)], axis=1)
        return y + (xin.reshape(seq, 8, 2 * LANES) * gains[None]).reshape(rows, 2 * LANES)

    def convolve(k, pair):
        if pair:
            wait_w(k, 0)
        else:
            wait_vg(k)
        v = rows_of(pair, 0)
        y = with_skip(long_filter(v.astype(BF16), 0, pair), 0, pair, v)
        if pair:
            wait_w(k, 1)
        gated = rows_of(pair, 1) * y
        y = with_skip(long_filter(gated.astype(BF16), 1, pair), 1, pair, gated)
        y = y.reshape(seq, 8, 2 * LANES)
        out = jnp.concatenate([y[:, :, :LANES], y[:, :, LANES:]], axis=1)
        out = out.astype(BF16)
        if k == 0:
            m_send[pair] = out
        else:
            for j in range(nx):
                m1_send[pair, :, j] = out[j * nz:(j + 1) * nz]

    def filter_spectra(f, pair):
        scale = 1.0 / (LANES * seq)
        cols = []
        for k in range(2):
            lo = 16 * pair + 8 * k
            cols.append(jnp.concatenate(
                [h[f, lo:lo + 8, LANES * a:LANES * a + LANES] for a in range(seq)], axis=0))
        outs = forward(jnp.concatenate(cols, axis=1).astype(BF16))
        for k in range(2):
            spec[f, 2 * pair + k] = outs[k] * scale

    def embed():
        token = lax.broadcasted_iota(jnp.int32, (LANES, LANES), 0)
        pos = me * LANES + lax.broadcasted_iota(jnp.int32, (LANES, LANES), 1)
        chain = jnp.zeros((LANES, LANES), jnp.int32)
        end = jnp.int32(0)
        for j in range(7):
            end = end + sizes_ref[j]
            chain = chain + jnp.where(pos >= end, 1, 0)
        vocab = amino_ref.shape[0]
        ids = jnp.broadcast_to(ids_ref[...], (LANES, LANES))
        hot = jnp.where(token < vocab, jnp.where(token == ids, 1.0, 0.0), jnp.where(token - vocab == chain, 1.0, 0.0))
        tab[...] = jnp.zeros_like(tab)
        tab[:vocab] = amino_ref[...].astype(F32)
        tab[vocab:vocab + 8] = poly_ref[...].astype(F32)
        emb[...] = dot(hot.astype(F32).T.astype(BF16), tab[...].astype(BF16)).astype(BF16)

    per = cw // CH

    def project(p, xx, normed):
        chunk = dot(normed, win[p, xx]).T.astype(BF16).reshape(per, 2, 16, LANES)
        vg_send[pl.ds(xx * per, per), p] = chunk[:, 0]
        w_send[p, pl.ds(xx * per, per)] = chunk[:, 1]

    def project_gate(j, normed):
        chunk = dot(normed, win[2, j]).T.astype(BF16).reshape(per, 2, 16, LANES)
        for half in range(2):
            g2t[j, half] = chunk[:, half].reshape(hw, LANES)

    def y_copy(half, xx, to):
        return pltpu.make_async_remote_copy(
            src_ref=hyt.at[half, xx], dst_ref=yall.at[0, half, x if to else xx],
            send_sem=y_s.at[half, xx], recv_sem=y_r.at[half, x if to else xx],
            device_id=(sec, xx, z), device_id_type=MESH)

    def make_hyena(k, half):
        hyena = m_recv[half].reshape(d // 2, LANES).astype(F32) * g2t[:, half].reshape(d // 2, LANES).astype(F32)
        if k == 0:
            hyt[half] = hyena.astype(BF16).reshape(nx, hw, LANES)
            for o in orders:
                if o:
                    y_copy(half, lax.rem(x + o, nx), True).start()
            yall[0, half, x] = hyt[half, x]
        return hyena.T.astype(BF16)

    def wait_y(half):
        for o in range(1, nx):
            y_copy(half, lax.rem(x + o, nx), False).wait_recv()

    def grad_of(step, half):
        y = jnp.concatenate([yall[step, half, j] for j in range(nx)], axis=1)
        half_d = d // 2
        for n in range(2):
            cols = slice(n * half_d, (n + 1) * half_d)
            s = jnp.concatenate([sall[step, j, :, cols] for j in range(nx)], axis=0)
            term = dot(y, s)
            if step == 0:
                part[half, :, cols] = term
            else:
                part[half, :, cols] = part[half, :, cols] + term

    def exit_rows(half, j):
        w = wout[j].reshape(seq, 2, 16, cw)
        return w[:, half].reshape(d // 2, cw)

    def half_exit(hyena_rows):
        for j in range(nx):
            acc[:, j * cw:(j + 1) * cw] = dot(hyena_rows, exit_rows(0, j))

    def normalize(values):
        return (values * lax.rsqrt(jnp.mean(values * values, axis=1, keepdims=True) + EPS) * gain_ref[...]).astype(BF16)

    def z_copy(half, zz, to):
        return pltpu.make_async_remote_copy(
            src_ref=rsend.at[half, zz], dst_ref=rrecv.at[half, z if to else zz], send_sem=z_s.at[half, zz],
            recv_sem=z_r.at[half, z if to else zz], device_id=(sec, x, zz), device_id_type=MESH)

    def send_partials(half):
        rsend[half] = part[half].astype(BF16).reshape(nz, 16, d)

        def one(i, carry):
            z_copy(half, lax.rem(z + far(i), nz), True).start()
            return carry

        lax.fori_loop(0, nz - 1, one, 0)
        grad_ref[16 * half:16 * half + 16] = part[half, pl.ds(pl.multiple_of(z * 16, 16), 16), :]

    def add_partials(half):
        def one(i, carry):
            zz = lax.rem(z + i, nz)
            z_copy(half, zz, False).wait_recv()
            grad_ref[16 * half:16 * half + 16] = grad_ref[16 * half:16 * half + 16] + rrecv[half, zz].astype(F32)
            return carry

        lax.fori_loop(1, nz, one, 0)

    def send_seeds(step):
        copies["seed", step].wait()
        seed_copy(step, 0).start()
        seed_copy(step, 1).start()

    def wait_seeds(step):
        for w in range(2):
            forward_arrival(step, w).wait_recv()

    def forward_seeds(step):
        for w in range(2):
            seed_arrival(step, w).wait_recv()
            forward_copy(step, w).start()

    def layer(k, normed):
        for xx, o in zip(columns, orders):
            for p in range(2):
                if k == 0:
                    copies["win", p, o].wait()
                project(p, xx, normed)
            if k == 0 and o == orders[0]:
                continue
            if k == 0 and o == orders[1]:
                pl.semaphore_wait(barrier, seq + 1)
                send_vg(k, orders[0])
            send_vg(k, o)
        for p in range(2):
            send_w(k, p)
        if k == 0:
            send_seeds(0)
            for j in range(nx):
                copies["win", 2, j].wait()
        for j in range(nx):
            project_gate(j, normed)
        if k == 1:
            send_gates()
            forward_seeds(0)
        if k == 0:
            for name in ("h", "fk", "tw", "g", "fi", "skip", "ids", "sizes", "amino", "poly"):
                copies[name].wait()
            for pair in range(2):
                for f in range(2):
                    filter_spectra(f, pair)
            embed()
        for half in range(2):
            convolve(k, half)
            send_mixed(k, half)
            if k == 1 and half == 0:
                forward_seeds(1)
        if k == 0:
            send_seeds(1)
            for j in range(nx):
                copies["wout", j].wait()
        else:
            wait_seeds(0)
            wait_y(0)
            grad_of(0, 0)
            wait_gates()
            for half in range(2):
                wait_along_z(half)
                send_on(half)
                hyena_along_x(half)
                if half == 0:
                    wait_seeds(1)
                grad_of(1, half)
                send_partials(half)
                if half == 0:
                    wait_y(1)
                    grad_of(0, 1)
        wait_mixed(k, 0)
        first_rows = make_hyena(k, 0)
        half_exit(first_rows)
        wait_mixed(k, 1)
        second_rows = make_hyena(k, 1)
        return second_rows

    def shift_copy(j):
        return pltpu.make_async_remote_copy(
            src_ref=hsend.at[j], dst_ref=hrecv.at[j], send_sem=sh_s.at[j], recv_sem=sh_r.at[j],
            device_id=(after, x, z), device_id_type=MESH)

    def start_shift(j):
        @pl.when(sec < ns - 1)
        def _():
            shift_copy(j).start()

    def wait_shift():
        @pl.when(sec > 0)
        def _():
            for j in range(nx):
                shift_copy(j).wait_recv()
            emb[...] = jnp.concatenate([hrecv[j] for j in range(nx)], axis=1)

    copies["x"].wait()
    copies["gain"].wait()
    first_normed = normalize(x_ref[...].astype(F32))
    hyena_rows = layer(0, first_normed)
    for j in range(0, nx, 2):
        cols = slice(j * cw, (j + 2) * cw)
        w = jnp.concatenate([exit_rows(1, j), exit_rows(1, j + 1)], axis=1)
        out = (x_ref[:, cols].astype(F32) + (acc[:, cols] + dot(hyena_rows, w))).astype(BF16)
        for i in range(2):
            hsend[j + i] = out[:, i * cw:(i + 1) * cw]
            start_shift(j + i)
    wait_sent(0)
    wait_shift()
    hyena_rows = layer(1, normalize(emb[...].astype(F32)))

    for j in range(nx):
        cols = slice(j * cw, (j + 1) * cw)
        out = emb[:, cols].astype(F32) + (acc[:, cols] + dot(hyena_rows, exit_rows(1, j)))
        passed_ref[:, cols] = out.astype(BF16)
    wait_sent(1)
    @pl.when(sec < ns - 1)
    def _():
        for j in range(nx):
            shift_copy(j).wait_send()

    for step in range(2):
        for w in range(2):
            seed_copy(step, w).wait_send()
            forward_copy(step, w).wait_send()
    for o in range(1, nx):
        xx = lax.rem(x + o, nx)
        gate_copy(xx, True).wait_send()
        for half in range(2):
            y_copy(half, xx, True).wait_send()
            on_copy(half, xx, True).wait_send()
    add_partials(0)
    add_partials(1)

    def z_drain(i, carry):
        for half in range(2):
            z_copy(half, lax.rem(z + i, nz), True).wait_send()
        return carry

    lax.fori_loop(1, nz, z_drain, 0)


def local(shape, resident, ids, sizes, amino, poly, gain, win, kernels, skips, wout, seeds):
    ns, nx, nz = shape
    seq = nx * nz
    d = CH * seq
    cw = CH * nz
    hw = cw // 2
    fk, fi, tw, g = dft_tables(seq)
    vmem = pl.BlockSpec(memory_space=pltpu.VMEM)
    hbm = pl.BlockSpec(memory_space=pl.ANY)
    dma = pltpu.SemaphoreType.DMA
    operands = (resident[0], ids.reshape(1, LANES), sizes, amino, poly, gain, win[0], kernels[0], skips[0], wout[0],
                seeds[0], fk, fi, tw, g)

    def like(i, space=pltpu.VMEM):
        return space(operands[i].shape, operands[i].dtype)

    passed, grad = pl.pallas_call(
        lambda *refs: body(ns, nx, nz, *refs),
        out_shape=(pltpu.VMEM((LANES, d), BF16), pltpu.VMEM((CH, d), F32)),
        in_specs=[hbm] * len(operands),
        out_specs=(vmem, vmem),
        scratch_shapes=[
            like(0), like(1), like(2, pltpu.SMEM), like(3), like(4), like(5), like(8, pltpu.SMEM),
            like(11), like(12), like(13), like(14),
            pltpu.VMEM((3, nx, d, cw), BF16),
            pltpu.VMEM((nx, d, cw), BF16),
            pltpu.VMEM((2, CH, LANES * seq), F32),
            pltpu.VMEM((2, 4, 8 * seq, 2 * LANES), F32),
            pltpu.VMEM((2, nx, LANES, d), BF16),
            pltpu.VMEM((seq, 2, 16, LANES), BF16),
            pltpu.VMEM((seq, 2, 16, LANES), BF16),
            pltpu.VMEM((2, seq, 16, LANES), BF16),
            pltpu.VMEM((2, seq, 16, LANES), BF16),
            pltpu.VMEM((2, seq, 16, LANES), BF16),
            pltpu.VMEM((2, seq, 16, LANES), BF16),
            pltpu.VMEM((2, nz, nx, 16, LANES), BF16),
            pltpu.VMEM((2, nz, nx, 16, LANES), BF16),
            pltpu.VMEM((nx, 2, hw, LANES), BF16),
            pltpu.VMEM((nx, 2, hw, LANES), BF16),
            pltpu.VMEM((2, nx, hw, LANES), BF16),
            pltpu.VMEM((2, 2, nx, hw, LANES), BF16),
            pltpu.VMEM((nx, LANES, cw), BF16),
            pltpu.VMEM((nx, LANES, cw), BF16),
            pltpu.VMEM((LANES, d), BF16),
            pltpu.VMEM((LANES, d), F32),
            pltpu.VMEM((LANES, d), F32),
            pltpu.VMEM((2, hw, d), F32),
            pltpu.VMEM((2, nz, 16, d), BF16),
            pltpu.VMEM((2, nz, 16, d), BF16),
            dma((4 * nx + 14,)),
            dma((2,)),
            dma((2,)),
            dma((2, 2)),
            dma((2, 2)),
            dma((2,)),
            dma((2,)),
            dma((2,)),
            dma((2,)),
            dma((2, nx)),
            dma((2, nx)),
            dma((nx,)),
            dma((nx,)),
            dma((nx,)),
            dma((nx,)),
            dma((2, nx)),
            dma((2, nx)),
            dma((2, 2)),
            dma((2, 2)),
            dma((2, 2)),
            dma((2, 2)),
            dma((2, nz)),
            dma((2, nz)),
        ],
        compiler_params=pltpu.CompilerParams(
            collective_id=0, has_side_effects=True, vmem_limit_bytes=66600000),
    )(*operands)

    def write(passed_ref, grad_ref, passed_out, grad_out, sems):
        copies = [pltpu.make_async_copy(passed_ref, passed_out.at[0], sems.at[0]),
                  pltpu.make_async_copy(grad_ref, grad_out.at[0], sems.at[1])]
        for c in copies:
            c.start()
        for c in copies:
            c.wait()

    return pl.pallas_call(
        write,
        out_shape=(jax.ShapeDtypeStruct((1, LANES, d), BF16), jax.ShapeDtypeStruct((1, CH, d), F32)),
        in_specs=[vmem, vmem],
        out_specs=(hbm, hbm),
        scratch_shapes=[dma((2,))],
    )(*(pltpu.with_memory_space_constraint(t, pltpu.VMEM) for t in (passed, grad)))


SEQ = ("seq_0", "seq_1")


def build(mesh, ns, nx, nz):
    torus = Mesh(mesh.devices.reshape(ns, nx, nz), ("section", "seq_0", "seq_1"))
    placed = (
        P("section", SEQ, None),
        P(SEQ),
        P(),
        P(),
        P(),
        P("section", None),
        P("section", None, None),
        P("section", None, SEQ, None),
        P("section", None, SEQ),
        P("section", None, None),
        P("section", None, SEQ, None),
    )
    return jax.shard_map(
        lambda *args: local((ns, nx, nz), *args),
        mesh=torus,
        in_specs=placed,
        out_specs=(P("section", SEQ, None), P("section", SEQ, None)),
        check_vma=False,
    )


def solution(mesh):
    return build(mesh, mesh.shape["section"], 4, 8)
```
